32 devices in a mesh: gx: 8 (over y, x, core), gy: 4 (over z).
Axes of the slice: x: 2, y: 2, z: 4, core: 2. Of those that a mesh axis runs over, the one named last changes fastest.
Arguments:
- basis: float32 [32, 64, 32, 256], P(None, 'gx', 'gy'), may hold values from -6 to 6
- rhs: float32 [64, 32, 256], P('gx', 'gy'), may hold values from -12 to 12
- extra_diag: float32 [64, 32, 256], P('gx', 'gy'), may hold values from 0.02 to 0.5
- coeff: float32 [3, 64, 32, 256], P(None, 'gx', 'gy'), may hold values from 0.3 to 3
Outputs:
- guess: float32 [64, 32, 256], P('gx', 'gy')
- stepped: float32 [64, 32, 256], P('gx', 'gy')
The draws below stay inside these ranges and needn't reach their ends.
All inputs are finite; a program needn't handle non-finite values.
Results may differ from the reference program's by a relative error of at most 0.0003.
Values sent between devices are 32-bit elements; how exact they have to be, the bound alone decides.
No kernel may reach another device: no remote copies, remote signals or barrier semaphores. Data moves between devices by JAX's collectives and lax.ppermute only.
A program may use at most 64 MiB of HBM per device.

```python
import math
import jax
import jax.numpy as jnp
from jax import lax

NZ = 256
NV = 32
NX = 64
NY = 32


def shared_fields(key):
    common_key = jax.random.fold_in(key, 101)
    latent_key = jax.random.fold_in(key, 102)
    own_key = jax.random.fold_in(key, 103)
    mixing_key = jax.random.fold_in(key, 104)
    factor_key = jax.random.fold_in(key, 105)
    noise_key = jax.random.fold_in(key, 106)
    latent_count = 8
    common = jnp.clip(jax.random.normal(common_key, (NX, NY, NZ), jnp.float32), -4.0, 4.0)
    latent = jnp.clip(jax.random.normal(latent_key, (latent_count, NX, NY, NZ), jnp.float32), -4.0, 4.0)
    own = jnp.clip(jax.random.normal(own_key, (NV, NX, NY, NZ), jnp.float32), -4.0, 4.0)
    noise_scale = 0.6
    mixing = jnp.clip(jax.random.normal(mixing_key, (NV, latent_count), jnp.float32), -3.0, 3.0) / math.sqrt(latent_count)
    vectors = common[None] + jnp.tensordot(mixing, latent, axes=1) + own
    vectors = jnp.clip(vectors, -6.0, 6.0)
    factors = jnp.clip(jax.random.normal(factor_key, (NV,), jnp.float32), -3.0, 3.0)
    noise = jnp.clip(jax.random.normal(noise_key, (NX, NY, NZ), jnp.float32), -6.0, 6.0)
    right = jnp.tensordot(factors, vectors, axes=1) / math.sqrt(NV) + noise_scale * noise
    return (vectors, jnp.clip(right, -12.0, 12.0))


def draw_basis(key, part):
    return shared_fields(key)[0]


def draw_rhs(key, part):
    return shared_fields(key)[1]


def block_levels(rng, extent, shards, smallest, high):
    factor_of = 1.0
    for axis_at, blocks in shards:
        steps = jax.random.uniform(jax.random.fold_in(jax.random.fold_in(rng, 6), axis_at), (blocks,), jnp.float32, smallest / len(shards), high / len(shards))
        factor_of = factor_of * jnp.repeat(jnp.exp(steps), extent[axis_at] // blocks).reshape((-1,) + (1,) * (len(extent) - 1 - axis_at))
    return factor_of


def setup_inputs(seed: int = 0) -> dict:
    arg_keys = jax.random.split(jax.random.key(seed), 5)
    basis = draw_basis(jax.random.fold_in(arg_keys[4], 71), 0)
    rhs = draw_rhs(jax.random.fold_in(arg_keys[4], 71), 0)
    extra_diag = jnp.clip(jnp.exp(math.log(0.5) - 3.218876 * jax.random.uniform(arg_keys[2], (NX, NY, NZ), jnp.float32) ** block_levels(arg_keys[2], (NX, NY, NZ), ((0, 8), (1, 4)), -0.2, 0.2)), 0.02, 0.5)
    coeff = jnp.clip(jnp.exp(math.log(3.0) - 2.3025851 * jax.random.uniform(arg_keys[3], (3, NX, NY, NZ), jnp.float32) ** block_levels(arg_keys[3], (3, NX, NY, NZ), ((1, 8), (2, 4)), -0.2, 0.2)), 0.3, 3.0)
    return {"basis": basis, "rhs": rhs, "extra_diag": extra_diag, "coeff": coeff}


precise = lax.Precision.HIGHEST

def flux_apply(padded, coeff_pad, extra):
    center = padded[:, 1:-1, 1:-1]
    coeff_mid = coeff_pad[:, 1:-1, 1:-1]
    flux_x = coeff_mid[0] * (center - padded[:, 2:, 1:-1])
    flux_y = coeff_mid[1] * (center - padded[:, 1:-1, 2:])
    below_x = coeff_pad[0, :-2, 1:-1] * (padded[:, :-2, 1:-1] - center)
    below_y = coeff_pad[1, 1:-1, :-2] * (padded[:, 1:-1, :-2] - center)
    next_z = jnp.concatenate([center[..., 1:], jnp.zeros_like(center[..., :1])], axis=-1)
    flux_z = coeff_mid[2] * (center - next_z)
    below_z = jnp.concatenate([jnp.zeros_like(flux_z[..., :1]), flux_z[..., :-1]], axis=-1)
    return extra * center + flux_x + flux_y + flux_z - below_x - below_y - below_z

def small_solve(matrix, vector):
    lower = jnp.linalg.cholesky(matrix)
    middle = lax.linalg.triangular_solve(lower, vector[:, None], left_side=True, lower=True)
    result = lax.linalg.triangular_solve(lower, middle, left_side=True, lower=True, transpose_a=True)
    return result[:, 0]

def reference(basis, rhs, extra_diag, coeff):
    coeff_pad = jnp.pad(coeff, ((0, 0), (1, 1), (1, 1), (0, 0)))

    def apply_one(field):
        padded = jnp.pad(field, ((1, 1), (1, 1), (0, 0)))
        return flux_apply(padded[None], coeff_pad, extra_diag)[0]
    applied = lax.map(apply_one, basis)
    flat_basis = basis.reshape(NV, -1)
    gram = jnp.dot(flat_basis, applied.reshape(NV, -1).T, precision=precise)
    gram = 0.5 * (gram + gram.T)
    projected = jnp.dot(flat_basis, rhs.reshape(-1), precision=precise)
    weights = small_solve(gram, projected)
    guess = jnp.tensordot(weights, basis, axes=1, precision=precise)
    residual = rhs - apply_one(guess)
    coeff_mid = coeff_pad[:, 1:-1, 1:-1]
    below_kz = jnp.concatenate([jnp.zeros_like(coeff[2][..., :1]), coeff[2][..., :-1]], axis=-1)
    diagonal = extra_diag + coeff_mid[0] + coeff_mid[1] + coeff_mid[2] + coeff_pad[0, :-2, 1:-1] + coeff_pad[1, 1:-1, :-2] + below_kz
    direction = residual / diagonal
    applied_dir = apply_one(direction)
    correction = jnp.dot(flat_basis, applied_dir.reshape(-1), precision=precise)
    shift_coef = small_solve(gram, correction)
    update = direction - jnp.tensordot(shift_coef, basis, axes=1, precision=precise)
    applied_upd = apply_one(update)
    step_size = jnp.sum(residual * update) / jnp.sum(update * applied_upd)
    return (guess, guess + step_size * update)
```

```python
import jax
import jax.numpy as jnp
from jax import lax
from jax.sharding import PartitionSpec as P

precise = lax.Precision.HIGHEST


def shifted(block, axis, distance):
    devices = range(lax.axis_size(axis))
    route = [(i - distance, i) for i in devices if i - distance in devices]
    return lax.ppermute(block, axis, route)


def padded_2(cells, sides, width):
    for axis, dim in sides:
        count = lax.axis_size(axis)
        ends = count - 1
        head = lax.slice_in_dim(cells, 0, width, axis=dim)
        tail = lax.slice_in_dim(cells, cells.shape[dim] - width, cells.shape[dim], axis=dim)
        cells = jnp.concatenate(
            [
                lax.ppermute(tail, axis, [(i, (i + 1) % count) for i in range(ends)]),
                cells,
                lax.ppermute(head, axis, [((i + 1) % count, i) for i in range(ends)]),
            ],
            axis=dim,
        )
    return cells


def sum_stages():
    wide, deep = lax.axis_size("gx"), lax.axis_size("gy")
    along_x = [(1 << k, 0) for k in range(wide.bit_length() - 1)]
    along_y = [(0, 1 << k) for k in range(deep.bit_length() - 1)]
    steps = along_y[:0:-1] + along_x + along_y[:1]
    single = len(steps) % 2
    stages = [[step] for step in steps[:single]]
    for at in range(single, len(steps), 2):
        (a, b), (c, d) = steps[at], steps[at + 1]
        stages.append([(a, b), (c, d), (a ^ c, b ^ d)])
    return stages


def sum_all(part):
    wide, deep = lax.axis_size("gx"), lax.axis_size("gy")
    if wide & (wide - 1) or deep & (deep - 1):
        return lax.psum(part, ("gx", "gy"))
    devices = [(i, j) for i in range(wide) for j in range(deep)]
    for stage in sum_stages():
        others = [
            lax.ppermute(
                part,
                ("gx", "gy"),
                [(i * deep + j, (i ^ a) * deep + (j ^ b)) for i, j in devices],
            )
            for a, b in stage
        ]
        for other in others:
            part = part + other
    return part


def flux_apply(padded, coeff_pad, extra):
    center = padded[:, 1:-1, 1:-1]
    coeff_mid = coeff_pad[:, 1:-1, 1:-1]
    flux_x = coeff_mid[0] * (center - padded[:, 2:, 1:-1])
    flux_y = coeff_mid[1] * (center - padded[:, 1:-1, 2:])
    below_x = coeff_pad[0, :-2, 1:-1] * (padded[:, :-2, 1:-1] - center)
    below_y = coeff_pad[1, 1:-1, :-2] * (padded[:, 1:-1, :-2] - center)
    next_z = jnp.concatenate([center[..., 1:], jnp.zeros_like(center[..., :1])], axis=-1)
    flux_z = coeff_mid[2] * (center - next_z)
    below_z = jnp.concatenate([jnp.zeros_like(flux_z[..., :1]), flux_z[..., :-1]], axis=-1)
    return extra * center + flux_x + flux_y + flux_z - below_x - below_y - below_z


def small_solve(matrix, vector):
    lower = jnp.linalg.cholesky(matrix)
    middle = lax.linalg.triangular_solve(lower, vector[:, None], left_side=True, lower=True)
    result = lax.linalg.triangular_solve(
        lower, middle, left_side=True, lower=True, transpose_a=True
    )
    return result[:, 0]


def on_device(basis, rhs, extra_diag, coeff):
    lower_x = shifted(coeff[0][-1:], "gx", 1)
    lower_y = shifted(coeff[1][:, -1:], "gy", 1)
    coeff_pad = jnp.pad(coeff, ((0, 0), (1, 1), (1, 1), (0, 0)))
    coeff_pad = coeff_pad.at[0, 0, 1:-1].set(lower_x[0])
    coeff_pad = coeff_pad.at[1, 1:-1, 0].set(lower_y[:, 0])
    count = basis.shape[0]
    flat_basis = basis.reshape(count, -1)
    padded_basis = padded_2(basis, (("gx", 1), ("gy", 2)), 1)
    applied = flux_apply(padded_basis, coeff_pad, extra_diag)
    local_gram = jnp.dot(flat_basis, applied.reshape(count, -1).T, precision=precise)
    local_proj = jnp.dot(flat_basis, rhs.reshape(-1), precision=precise)
    total = sum_all(jnp.concatenate([local_gram, local_proj[:, None]], axis=1))
    gram, projected = total[:, :count], total[:, count]
    gram = 0.5 * (gram + gram.T)
    weights = small_solve(gram, projected)
    guess = jnp.tensordot(weights, basis, axes=1, precision=precise)
    residual = rhs - jnp.tensordot(weights, applied, axes=1, precision=precise)
    coeff_mid = coeff_pad[:, 1:-1, 1:-1]
    below_kz = jnp.concatenate([jnp.zeros_like(coeff[2][..., :1]), coeff[2][..., :-1]], axis=-1)
    diagonal = (
        extra_diag
        + coeff_mid[0]
        + coeff_mid[1]
        + coeff_mid[2]
        + coeff_pad[0, :-2, 1:-1]
        + coeff_pad[1, 1:-1, :-2]
        + below_kz
    )
    direction = residual / diagonal
    direction_pad = padded_2(direction, (("gx", 0), ("gy", 1)), 1)
    applied_dir = flux_apply(direction_pad[None], coeff_pad, extra_diag)[0]
    local_corr = jnp.dot(flat_basis, applied_dir.reshape(-1), precision=precise)
    local_sums = jnp.stack([jnp.sum(residual * direction), jnp.sum(direction * applied_dir)])
    total = sum_all(jnp.concatenate([local_corr, local_sums])[None])[0]
    correction, numerator, curvature = total[:count], total[count], total[count + 1]
    shift_coef = small_solve(gram, correction)
    update = direction - jnp.tensordot(shift_coef, basis, axes=1, precision=precise)
    denominator = curvature - jnp.dot(correction, shift_coef, precision=precise)
    step_size = numerator / denominator
    return (guess, guess + step_size * update)


def solution(mesh):
    placed = (
        P(None, "gx", "gy", None),
        P("gx", "gy", None),
        P("gx", "gy", None),
        P(None, "gx", "gy", None),
    )
    return jax.shard_map(
        on_device,
        mesh=mesh,
        in_specs=placed,
        out_specs=(P("gx", "gy", None), P("gx", "gy", None)),
        check_vma=False,
    )
```

```python
import functools
import jax
import jax.numpy as jnp
from jax import lax
from jax.experimental import pallas as pl
from jax.experimental.pallas import tpu as pltpu
from jax.sharding import PartitionSpec as P

F32 = jnp.float32
BF16 = jnp.bfloat16
EXTRA = 16
LANES = 128
VM = pl.BlockSpec(memory_space=pltpu.VMEM)
RAW = pl.BlockSpec(memory_space=pl.ANY)
SM = pl.BlockSpec(memory_space=pltpu.SMEM)


def shape(*dims, dtype=F32):
    return jax.ShapeDtypeStruct(dims, dtype)


def call(body, outs, ins, scratch=(), limit=24, work=0, moved=0):
    return pl.pallas_call(
        body,
        out_shape=outs,
        in_specs=ins,
        out_specs=jax.tree.map(lambda _: VM, outs),
        scratch_shapes=list(scratch),
        compiler_params=pltpu.CompilerParams(vmem_limit_bytes=limit << 20),
        cost_estimate=pl.CostEstimate(flops=work, bytes_accessed=moved, transcendentals=0),
    )


def sum_stages():
    wide, deep = lax.axis_size("gx"), lax.axis_size("gy")
    along_x = [(1 << k, 0) for k in range(wide.bit_length() - 1)]
    along_y = [(0, 1 << k) for k in range(deep.bit_length() - 1)]
    steps = along_y[:0:-1] + along_x + along_y[:1]
    single = len(steps) % 2
    stages = [[step] for step in steps[:single]]
    for at in range(single, len(steps), 2):
        (a, b), (c, d) = steps[at], steps[at + 1]
        stages.append([(a, b), (c, d), (a ^ c, b ^ d)])
    return stages


def sum_all(part):
    wide, deep = lax.axis_size("gx"), lax.axis_size("gy")
    if wide & (wide - 1) or deep & (deep - 1):
        return lax.psum(part, ("gx", "gy"))
    devices = [(i, j) for i in range(wide) for j in range(deep)]
    for stage in sum_stages():
        others = [
            lax.ppermute(
                part,
                ("gx", "gy"),
                [(i * deep + j, (i ^ a) * deep + (j ^ b)) for i, j in devices],
            )
            for a, b in stage
        ]
        for other in others:
            part = part + other
    return part


def send(block, axis, step):
    size = lax.axis_size(axis)
    return lax.ppermute(block, axis, [(i, i + step) for i in range(size) if 0 <= i + step < size])


def halves(value):
    high = value.astype(BF16)
    return high, (value - high.astype(F32)).astype(BF16)


def put(stack, at, value, extra=None):
    count, deep = value.shape
    lanes = pl.ds(at * deep, deep)
    high, low = halves(value)
    stack[pl.ds(0, count), lanes] = high
    stack[pl.ds(count, count), lanes] = low
    if extra is not None:
        high, low = halves(extra)
        row = lax.broadcasted_iota(jnp.int32, (EXTRA, deep), 0)
        both = jnp.where(row == 0, high.astype(F32), jnp.where(row == 1, low.astype(F32), 0.0))
        stack[pl.ds(2 * count, EXTRA), lanes] = both.astype(BF16)


def by_rows(left, right):
    return lax.dot_general(left, right, (((1,), (1,)), ((), ())), preferred_element_type=F32)


def fold_rows(full, count):
    top = full[:count] + full[count : 2 * count]
    if full.shape[0] == 2 * count:
        return top
    last = full[2 * count : 2 * count + 1] + full[2 * count + 1 : 2 * count + 2]
    return jnp.concatenate([top, jnp.broadcast_to(last, (8, full.shape[1]))], axis=0)


def fold(full, count):
    rows = fold_rows(full, count)
    body = rows[:, :count] + rows[:, count : 2 * count]
    last = rows[:, 2 * count : 2 * count + 1] + rows[:, 2 * count + 1 : 2 * count + 2]
    return body, last


def faces_kernel(basis, coeff, up_x, down_x, up_y, down_y, sems):
    count, nx, ny, deep = basis.shape
    moves = []
    for y in range(ny):
        rows = pl.ds(y * count, count)
        moves.append((basis.at[:, nx - 1, y, :], up_x.at[rows]))
        moves.append((basis.at[:, 0, y, :], down_x.at[rows]))
    for x in range(nx):
        rows = pl.ds(x * count, count)
        moves.append((basis.at[:, x, ny - 1, :], up_y.at[rows]))
        moves.append((basis.at[:, x, 0, :], down_y.at[rows]))
    moves.append((coeff.at[0, nx - 1], up_x.at[pl.ds(ny * count, ny)]))
    moves.append((coeff.at[1, :, ny - 1, :], up_y.at[pl.ds(nx * count, nx)]))
    copies = [pltpu.make_async_copy(a, b, sems.at[k]) for k, (a, b) in enumerate(moves)]
    for copy in copies:
        copy.start()
    for copy in copies:
        copy.wait()


def faces(basis, coeff):
    count, nx, ny, deep = basis.shape
    outs = (
        shape(ny * count + ny, deep),
        shape(ny * count, deep),
        shape(nx * count + nx, deep),
        shape(nx * count, deep),
    )
    sems = pltpu.SemaphoreType.DMA((2 * nx + 2 * ny + 2,))
    return call(faces_kernel, outs, [RAW, RAW], [sems], limit=4)(basis, coeff)


def row(ref, *at):
    return ref[at[:-1] + (pl.ds(at[-1], 1), slice(None))]


def near_z(field, upper, lower):
    deep = field.shape[1]
    above, below = pltpu.roll(field, deep - 1, 1), pltpu.roll(field, 1, 1)
    return upper * above + lower * below


def inner_kernel(basis, coeff, extra, cols, inner, stack, upper, lower, diag, sems):
    nx, ny, count, deep = cols.shape
    copies = []
    for x in range(nx):
        for y in range(ny):
            copies.append(
                pltpu.make_async_copy(basis.at[:, x, y, :], cols.at[x, y], sems.at[x * ny + y])
            )
            copies[-1].start()
    level = lax.broadcasted_iota(jnp.int32, (ny, deep), 0)
    lane = lax.broadcasted_iota(jnp.int32, (ny, deep), 1)
    for x in range(nx):
        cz = coeff[2, x]
        upper[x] = jnp.where(lane == deep - 1, 0.0, cz)
        under = jnp.where(lane == 0, 0.0, pltpu.roll(cz, 1, 1))
        lower[x] = under
        cy = coeff[1, x]
        total = extra[x] + coeff[0, x] + cy + cz + under
        total = total + jnp.where(level == 0, 0.0, pltpu.roll(cy, 1, 0))
        if x:
            total = total + coeff[0, x - 1]
        diag[x] = total
    for copy in copies:
        copy.wait()
    for x in range(nx):
        for y in range(ny):
            here = cols[x, y]
            sums = near_z(here, row(upper, x, y), row(lower, x, y))
            if x + 1 < nx:
                sums += row(coeff, 0, x, y) * cols[x + 1, y]
            if x:
                sums += row(coeff, 0, x - 1, y) * cols[x - 1, y]
            if y + 1 < ny:
                sums += row(coeff, 1, x, y) * cols[x, y + 1]
            if y:
                sums += row(coeff, 1, x, y - 1) * cols[x, y - 1]
            inner[x, y] = row(diag, x, y) * here - sums
            put(stack, x * ny + y, here)


def inside(basis, coeff, extra):
    count, nx, ny, deep = basis.shape
    cells = nx * ny * deep
    outs = (shape(nx, ny, count, deep), shape(nx, ny, count, deep), shape(2 * count, cells, dtype=BF16))
    small = pltpu.VMEM((nx, ny, deep), F32)
    sems = pltpu.SemaphoreType.DMA((nx * ny,))
    return call(
        inner_kernel, outs, [RAW, VM, VM], [small, small, small, sems],
        work=20 * count * cells, moved=16 * count * cells,
    )(basis, coeff, extra)


def inverse_diagonal(coeff, extra, from_left, from_front, count, x):
    nx, ny, deep = extra.shape
    level = lax.broadcasted_iota(jnp.int32, (ny, deep), 0)
    lane = lax.broadcasted_iota(jnp.int32, (ny, deep), 1)
    cy, cz = coeff[1, x], coeff[2, x]
    total = extra[x] + coeff[0, x] + cy + cz
    total += jnp.where(lane == 0, 0.0, pltpu.roll(cz, 1, 1))
    front = from_front[pl.ds(nx * count + x, 1), :]
    total += jnp.where(level == 0, front, pltpu.roll(cy, 1, 0))
    total += coeff[0, x - 1] if x else from_left[pl.ds(ny * count, ny), :]
    return 1.0 / total


def full_value(cols, inner, coeff, left, right, front, back, x, y):
    nx, ny, count, deep = cols.shape
    value = inner[x, y]
    of_x, of_y = pl.ds(y * count, count), pl.ds(x * count, count)
    if x == 0:
        value += left[pl.ds(ny * count + y, 1), :] * (cols[x, y] - left[of_x])
    if x == nx - 1:
        value -= row(coeff, 0, x, y) * right[of_x]
    if y == 0:
        value += front[pl.ds(nx * count + x, 1), :] * (cols[x, y] - front[of_y])
    if y == ny - 1:
        value -= row(coeff, 1, x, y) * back[of_y]
    return value


def border_kernel(odd, cols, inner, coeff, extra, rhs, left, right, front, back, face_x, face_y, scale):
    nx, ny, count, deep = cols.shape
    for x in range(nx):
        scale[x] = inverse_diagonal(coeff, extra, left, front, count, x)
    value = functools.partial(full_value, cols, inner, coeff, left, right, front, back)
    for y in range(ny):
        face_x[pl.ds(y * count, count), :] = value(0, y) * row(scale, 0, y)
    face_x[pl.ds(ny * count, ny), :] = scale[0] * rhs[0]

    def side(y):
        for x in range(nx):
            face_y[pl.ds(x * count, count), :] = value(x, y) * row(scale, x, y)
            face_y[pl.ds(nx * count + x, 1), :] = row(scale, x, y) * row(rhs, x, y)

    @pl.when(odd[0] == 0)
    def _():
        side(0)

    @pl.when(odd[0] == 1)
    def _():
        side(ny - 1)


def border(odd, cols, inner, coeff, extra, rhs, halo):
    nx, ny, count, deep = cols.shape
    outs = (shape(ny * count + ny, deep), shape(nx * count + nx, deep))
    return call(
        border_kernel, outs, [SM] + [VM] * 9, [pltpu.VMEM((nx, ny, deep), F32)], limit=10
    )(odd, cols, inner, coeff, extra, rhs, *halo)


def local_kernel(
    cols, inner, basis_stack, coeff, extra, rhs, left, right, front, back,
    part, scaled_stack, value_stack, pair_stack, scaled, scale, upper, scaled_rhs,
):
    nx, ny, count, deep = cols.shape
    lane = lax.broadcasted_iota(jnp.int32, (ny, deep), 1)
    for x in range(nx):
        inverse = inverse_diagonal(coeff, extra, left, front, count, x)
        scale[x] = inverse
        scaled_rhs[x] = inverse * rhs[x]
        upper[x] = jnp.where(lane == deep - 1, 0.0, coeff[2, x])
    for x in range(nx):
        for y in range(ny):
            value = full_value(cols, inner, coeff, left, right, front, back, x, y)
            result = value * row(scale, x, y)
            scaled[x, y] = result
            put(value_stack, x * ny + y, value, row(rhs, x, y))
            put(scaled_stack, x * ny + y, result, row(scaled_rhs, x, y))
    for x in range(nx):
        for y in range(ny):
            over, ahead = row(upper, x, y), pltpu.roll(scaled[x, y], deep - 1, 1)
            pair = over * ahead
            pair_rhs = over * pltpu.roll(jnp.broadcast_to(row(scaled_rhs, x, y), (8, deep)), deep - 1, 1)[:1]
            if x + 1 < nx:
                pair += row(coeff, 0, x, y) * scaled[x + 1, y]
                pair_rhs += row(coeff, 0, x, y) * row(scaled_rhs, x + 1, y)
            if y + 1 < ny:
                pair += row(coeff, 1, x, y) * scaled[x, y + 1]
                pair_rhs += row(coeff, 1, x, y) * row(scaled_rhs, x, y + 1)
            put(pair_stack, x * ny + y, pair, pair_rhs)
    gram, projected = fold(by_rows(basis_stack[...], value_stack[...]), count)
    square, square_rhs = fold(by_rows(value_stack[...], scaled_stack[...]), count)
    pairs, pairs_rhs = fold(by_rows(scaled_stack[...], pair_stack[...]), count)
    part[...] = jnp.zeros_like(part)
    part[pl.ds(0, count), pl.ds(0, count)] = gram
    part[:, pl.ds(count, count)] = square
    part[:, pl.ds(2 * count, count)] = pairs
    part[pl.ds(0, count), pl.ds(3 * count, 1)] = projected
    part[:, pl.ds(3 * count + 1, 1)] = square_rhs
    part[:, pl.ds(3 * count + 2, 1)] = pairs_rhs


def local_sums(cols, inner, basis_stack, coeff, extra, rhs, halo):
    nx, ny, count, deep = cols.shape
    cells = nx * ny * deep
    tall = 2 * count + EXTRA
    small = pltpu.VMEM((nx, ny, deep), F32)
    outs = (shape(count + 8, -(-(3 * count + 3) // LANES) * LANES), shape(tall, cells, dtype=BF16))
    return call(
        local_kernel,
        outs,
        [VM] * 10,
        [
            pltpu.VMEM((tall, cells), BF16),
            pltpu.VMEM((tall, cells), BF16),
            pltpu.VMEM((nx, ny, count, deep), F32),
            small, small, small,
        ],
        limit=28,
        work=60 * count * cells,
        moved=24 * count * cells,
    )(cols, inner, basis_stack, coeff, extra, rhs, *halo)


def shared_kernel(odd, part, scaled_stack, coeff, front, far_x, far_y, total, mine, pair_stack):
    count = part.shape[0] - 8
    nx, ny, deep = coeff.shape[1:]
    for y in range(ny):
        face = row(coeff, 0, nx - 1, y)
        put(
            pair_stack, y, face * far_x[pl.ds(y * count, count), :],
            face * far_x[pl.ds(ny * count + y, 1), :],
        )
        mine[:, pl.ds(y * deep, deep)] = scaled_stack[:, pl.ds(((nx - 1) * ny + y) * deep, deep)]
    for x in range(nx):
        own = front[pl.ds(nx * count + x, 1), :]
        face = jnp.where(odd[0] == 0, row(coeff, 1, x, ny - 1), own)
        put(
            pair_stack, ny + x, face * far_y[pl.ds(x * count, count), :],
            face * far_y[pl.ds(nx * count + x, 1), :],
        )

    def side(y):
        for x in range(nx):
            mine[:, pl.ds((ny + x) * deep, deep)] = scaled_stack[:, pl.ds((x * ny + y) * deep, deep)]

    @pl.when(odd[0] == 0)
    def _():
        side(ny - 1)

    @pl.when(odd[0] == 1)
    def _():
        side(0)

    pairs, pairs_rhs = fold(by_rows(mine[...], pair_stack[...]), count)
    total[...] = part[...]
    total[:, pl.ds(2 * count, count)] += pairs
    total[:, pl.ds(3 * count + 2, 1)] += pairs_rhs


def shared_sums(odd, part, scaled_stack, coeff, front, far_x, far_y):
    nx, ny, deep = coeff.shape[1:]
    wide = pltpu.VMEM((scaled_stack.shape[0], (nx + ny) * deep), BF16)
    return call(
        shared_kernel, shape(*part.shape), [SM] + [VM] * 6, [wide, wide], limit=12
    )(odd, part, scaled_stack, coeff, front, far_x, far_y)


def finish_kernel(total, basis_stack, scaled_stack, guess, stepped):
    count = total.shape[0] - 8
    nx, ny, deep = guess.shape
    sums = total[pl.ds(0, count), :]
    work = sums
    level = lax.broadcasted_iota(jnp.int32, (count, 1), 0)
    for k in range(count):
        line = work[k : k + 1, :] / work[k : k + 1, k : k + 1]
        column = work[:, k : k + 1]
        work = jnp.where(level == k, line, work - column * line)
    at = 3 * count
    turned = work.T
    weights = work[:, at : at + 1]
    weights_row = turned[at : at + 1, :]
    shift_row = turned[at + 1 : at + 2, :] - jnp.sum(weights * turned[count : 2 * count, :], axis=0, keepdims=True)
    sums_row = sums.T
    rhs_row = sums_row[at + 1 : at + 2, :]
    both = jnp.sum(weights * sums, axis=0, keepdims=True)
    correction = rhs_row - both[:, count : 2 * count]
    along = jnp.sum(weights_row * (rhs_row + correction), axis=1, keepdims=True)
    tail = total[pl.ds(count, 1), :]
    size = tail[:, at + 1 : at + 2] - along
    crossing = jnp.sum(
        weights_row * (both[:, 2 * count : at] - sums_row[at + 2 : at + 3, :] - tail[:, 2 * count : at]),
        axis=1, keepdims=True,
    ) + tail[:, at + 2 : at + 3]
    lost = jnp.sum(correction * shift_row, axis=1, keepdims=True)
    step = size / (size - 2.0 * crossing - lost)
    first = lax.broadcasted_iota(jnp.int32, (EXTRA, count), 0)
    of_basis = jnp.where(first == 0, weights_row, jnp.where(first == 1, weights_row - step * shift_row, 0.0))
    of_scaled = jnp.where(first == 1, -step * weights_row, 0.0)
    last = lax.broadcasted_iota(jnp.int32, (EXTRA, EXTRA), 0)
    place = lax.broadcasted_iota(jnp.int32, (EXTRA, EXTRA), 1)
    of_rhs = jnp.where((last == 1) & (place < 2), step, 0.0)
    basis_high, basis_low = halves(jnp.concatenate([of_basis, of_basis], axis=1))
    scaled_high, scaled_low = halves(jnp.concatenate([of_scaled, of_scaled, of_rhs], axis=1))
    for x in range(nx):
        lanes = pl.ds(x * ny * deep, ny * deep)
        fields = basis_stack[:, lanes]
        result = jnp.dot(basis_high, fields, preferred_element_type=F32)
        result += jnp.dot(basis_low, fields, preferred_element_type=F32)
        fields = scaled_stack[:, lanes]
        result += jnp.dot(scaled_high, fields, preferred_element_type=F32)
        result += jnp.dot(scaled_low, fields, preferred_element_type=F32)
        for y in range(ny):
            guess[x, pl.ds(y, 1), :] = result[0:1, y * deep : (y + 1) * deep]
            stepped[x, pl.ds(y, 1), :] = result[1:2, y * deep : (y + 1) * deep]


def finish(total, basis_stack, scaled_stack, block):
    return call(finish_kernel, (shape(*block),) * 2, [VM] * 3, limit=24)(
        total, basis_stack, scaled_stack
    )


def on_device(basis, rhs, extra_diag, coeff):
    odd = lax.axis_index("gx") % 2
    odd = odd.astype(jnp.int32).reshape(1)
    up_x, down_x, up_y, down_y = faces(basis, coeff)
    front, back = send(up_y, "gy", 1), send(down_y, "gy", -1)
    left, right = send(up_x, "gx", 1), send(down_x, "gx", -1)
    cols, inner, basis_stack = inside(basis, coeff, extra_diag)
    halo = (left, right, front, back)
    face_x, face_y = border(odd, cols, inner, coeff, extra_diag, rhs, halo)
    wide, deep = lax.axis_size("gx"), lax.axis_size("gy")
    route = []
    for i in range(wide):
        step = 1 if i % 2 else -1
        route += [(i * deep + j, i * deep + j + step) for j in range(deep) if 0 <= j + step < deep]
    far_y = lax.ppermute(face_y, ("gx", "gy"), route)
    far_x = send(face_x, "gx", -1)
    part, scaled_stack = local_sums(cols, inner, basis_stack, coeff, extra_diag, rhs, halo)
    part = shared_sums(odd, part, scaled_stack, coeff, front, far_x, far_y)
    total = sum_all(part)
    return finish(total, basis_stack, scaled_stack, rhs.shape)


def solution(mesh):
    placed = (
        P(None, "gx", "gy", None),
        P("gx", "gy", None),
        P("gx", "gy", None),
        P(None, "gx", "gy", None),
    )
    return jax.shard_map(
        on_device,
        mesh=mesh,
        in_specs=placed,
        out_specs=(P("gx", "gy", None), P("gx", "gy", None)),
        check_vma=False,
    )
```

```python
import functools
import jax
import jax.numpy as jnp
from jax import lax
from jax.experimental import pallas as pl
from jax.experimental.pallas import tpu as pltpu
from jax.sharding import PartitionSpec as P

F32 = jnp.float32
BF16 = jnp.bfloat16
EXTRA = 16
LANES = 128
VM = pl.BlockSpec(memory_space=pltpu.VMEM)
RAW = pl.BlockSpec(memory_space=pl.ANY)
SM = pl.BlockSpec(memory_space=pltpu.SMEM)


def shape(*dims, dtype=F32):
    return jax.ShapeDtypeStruct(dims, dtype)


def call(body, outs, ins, scratch=(), limit=24, work=0, moved=0):
    return pl.pallas_call(
        body,
        out_shape=outs,
        in_specs=ins,
        out_specs=jax.tree.map(lambda _: VM, outs),
        scratch_shapes=list(scratch),
        compiler_params=pltpu.CompilerParams(vmem_limit_bytes=limit << 20),
        cost_estimate=pl.CostEstimate(flops=work, bytes_accessed=moved, transcendentals=0),
    )


def sum_stages():
    wide, deep = lax.axis_size("gx"), lax.axis_size("gy")
    along_x = [(1 << k, 0) for k in range(wide.bit_length() - 1)]
    along_y = [(0, 1 << k) for k in range(deep.bit_length() - 1)]
    steps = along_y[:0:-1] + along_x + along_y[:1]
    single = len(steps) % 2
    stages = [[step] for step in steps[:single]]
    for at in range(single, len(steps), 2):
        (a, b), (c, d) = steps[at], steps[at + 1]
        stages.append([(a, b), (c, d), (a ^ c, b ^ d)])
    return stages


def sum_all(part):
    wide, deep = lax.axis_size("gx"), lax.axis_size("gy")
    if wide & (wide - 1) or deep & (deep - 1):
        return lax.psum(part, ("gx", "gy"))
    devices = [(i, j) for i in range(wide) for j in range(deep)]
    for stage in sum_stages():
        others = [
            lax.ppermute(
                part,
                ("gx", "gy"),
                [(i * deep + j, (i ^ a) * deep + (j ^ b)) for i, j in devices],
            )
            for a, b in stage
        ]
        for other in others:
            part = part + other
    return part


def send(block, axis, step):
    size = lax.axis_size(axis)
    return lax.ppermute(block, axis, [(i, i + step) for i in range(size) if 0 <= i + step < size])


def swap(block, axis, start):
    size = lax.axis_size(axis)
    pairs = [(i, i + 1) for i in range(start, size - 1, 2)]
    return lax.ppermute(block, axis, pairs + [(j, i) for i, j in pairs])


def halves(value):
    high = value.astype(BF16)
    return high, (value - high.astype(F32)).astype(BF16)


def put(stack, at, value, extra=None):
    count, deep = value.shape
    lanes = pl.ds(at * deep, deep)
    high, low = halves(value)
    stack[pl.ds(0, count), lanes] = high
    stack[pl.ds(count, count), lanes] = low
    if extra is not None:
        high, low = halves(extra)
        row = lax.broadcasted_iota(jnp.int32, (EXTRA, deep), 0)
        both = jnp.where(row == 0, high.astype(F32), jnp.where(row == 1, low.astype(F32), 0.0))
        stack[pl.ds(2 * count, EXTRA), lanes] = both.astype(BF16)


def by_rows(left, right):
    return lax.dot_general(left, right, (((1,), (1,)), ((), ())), preferred_element_type=F32)


def fold_rows(full, count):
    top = full[:count] + full[count : 2 * count]
    if full.shape[0] == 2 * count:
        return top
    last = full[2 * count : 2 * count + 1] + full[2 * count + 1 : 2 * count + 2]
    return jnp.concatenate([top, jnp.broadcast_to(last, (8, full.shape[1]))], axis=0)


def fold(full, count):
    rows = fold_rows(full, count)
    body = rows[:, :count] + rows[:, count : 2 * count]
    last = rows[:, 2 * count : 2 * count + 1] + rows[:, 2 * count + 1 : 2 * count + 2]
    return body, last


def faces_kernel(odd, basis, coeff, first_x, second_x, first_y, second_y, sems):
    count, nx, ny, deep = basis.shape
    first, second = (nx - 1) * (1 - odd[0]), (nx - 1) * odd[0]
    moves = []
    for x in range(nx):
        rows = pl.ds(x * count, count)
        moves.append((basis.at[:, x, ny - 1, :], first_y.at[rows], basis.at[:, x, 0, :]))
        moves.append((basis.at[:, x, 0, :], second_y.at[rows], basis.at[:, x, ny - 1, :]))
    sided = len(moves)
    for y in range(ny):
        rows = pl.ds(y * count, count)
        moves.append((basis.at[:, first, y, :], first_x.at[rows], None))
        moves.append((basis.at[:, second, y, :], second_x.at[rows], None))
    for target in (first_x, second_x):
        moves.append((coeff.at[0, nx - 1], target.at[pl.ds(ny * count, ny)], None))
    for target in (first_y, second_y):
        moves.append((coeff.at[1, :, ny - 1, :], target.at[pl.ds(nx * count, nx)], None))

    @pl.when(odd[1] == 0)
    def _():
        for k, (source, target, _) in enumerate(moves[:sided]):
            pltpu.make_async_copy(source, target, sems.at[k]).start()

    @pl.when(odd[1] == 1)
    def _():
        for k, (_, target, source) in enumerate(moves[:sided]):
            pltpu.make_async_copy(source, target, sems.at[k]).start()

    copies = [pltpu.make_async_copy(a, b, sems.at[k]) for k, (a, b, _) in enumerate(moves)]
    for copy in copies[sided:]:
        copy.start()
    for copy in copies:
        copy.wait()


def faces(odd, basis, coeff):
    count, nx, ny, deep = basis.shape
    of_x, of_y = shape(ny * count + ny, deep), shape(nx * count + nx, deep)
    sems = pltpu.SemaphoreType.DMA((2 * nx + 2 * ny + 4,))
    return call(faces_kernel, (of_x, of_x, of_y, of_y), [SM, RAW, RAW], [sems], limit=60)(odd, basis, coeff)


def row(ref, *at):
    return ref[at[:-1] + (pl.ds(at[-1], 1), slice(None))]


def near_z(field, upper, lower):
    deep = field.shape[1]
    above, below = pltpu.roll(field, deep - 1, 1), pltpu.roll(field, 1, 1)
    return upper * above + lower * below


def inner_kernel(basis, coeff, extra_raw, cols, inner, stack, diag, upper, lower, extra, sems):
    nx, ny, count, deep = cols.shape
    extra_copy = pltpu.make_async_copy(extra_raw, extra, sems.at[nx * ny])
    extra_copy.start()
    copies = []
    for x in range(nx):
        for y in range(ny):
            copies.append(
                pltpu.make_async_copy(basis.at[:, x, y, :], cols.at[x, y], sems.at[x * ny + y])
            )
            copies[-1].start()
    level = lax.broadcasted_iota(jnp.int32, (ny, deep), 0)
    lane = lax.broadcasted_iota(jnp.int32, (ny, deep), 1)
    extra_copy.wait()
    for x in range(nx):
        cz = coeff[2, x]
        upper[x] = jnp.where(lane == deep - 1, 0.0, cz)
        under = jnp.where(lane == 0, 0.0, pltpu.roll(cz, 1, 1))
        lower[x] = under
        cy = coeff[1, x]
        total = extra[x] + coeff[0, x] + cy + cz + under
        total = total + jnp.where(level == 0, 0.0, pltpu.roll(cy, 1, 0))
        if x:
            total = total + coeff[0, x - 1]
        diag[x] = total
    for copy in copies[:ny]:
        copy.wait()
    for x in range(nx):
        for copy in copies[(x + 1) * ny : (x + 2) * ny]:
            copy.wait()
        for y in range(ny):
            here = cols[x, y]
            sums = near_z(here, row(upper, x, y), row(lower, x, y))
            if x + 1 < nx:
                sums += row(coeff, 0, x, y) * cols[x + 1, y]
            if x:
                sums += row(coeff, 0, x - 1, y) * cols[x - 1, y]
            if y + 1 < ny:
                sums += row(coeff, 1, x, y) * cols[x, y + 1]
            if y:
                sums += row(coeff, 1, x, y - 1) * cols[x, y - 1]
            inner[x, y] = row(diag, x, y) * here - sums
            put(stack, x * ny + y, here)


def inside(basis, coeff, extra):
    count, nx, ny, deep = basis.shape
    cells = nx * ny * deep
    full = shape(nx, ny, count, deep)
    outs = (full, full, shape(2 * count, cells, dtype=BF16), shape(nx, ny, deep))
    small = pltpu.VMEM((nx, ny, deep), F32)
    sems = pltpu.SemaphoreType.DMA((nx * ny + 1,))
    return call(
        inner_kernel, outs, [RAW, VM, RAW], [small, small, small, sems],
        work=20 * count * cells, moved=16 * count * cells,
    )(basis, coeff, extra)


class Halo:
    def __init__(self, odd, refs):
        self.odd = odd
        self.refs = refs

    def rows(self, axis, upper, start, size):
        first, second = self.refs[2 * axis : 2 * axis + 2]
        here = pl.ds(start, size)
        return jnp.where(self.odd[axis] == (0 if upper else 1), first[here, :], second[here, :])


def inverse_diagonal(diag, halo, count, x):
    nx, ny, deep = diag.shape
    level = lax.broadcasted_iota(jnp.int32, (ny, deep), 0)
    total = diag[x] + jnp.where(level == 0, halo.rows(1, False, nx * count + x, 1), 0.0)
    if x == 0:
        total += halo.rows(0, False, ny * count, ny)
    return 1.0 / total


def full_value(cols, inner, coeff, halo, x, y):
    nx, ny, count, deep = cols.shape
    value = inner[x, y]
    if x == 0:
        value += halo.rows(0, False, ny * count + y, 1) * (cols[x, y] - halo.rows(0, False, y * count, count))
    if x == nx - 1:
        value -= row(coeff, 0, x, y) * halo.rows(0, True, y * count, count)
    if y == 0:
        value += halo.rows(1, False, nx * count + x, 1) * (cols[x, y] - halo.rows(1, False, x * count, count))
    if y == ny - 1:
        value -= row(coeff, 1, x, y) * halo.rows(1, True, x * count, count)
    return value


def border_kernel(odd, cols, inner, coeff, diag, rhs, xa, xb, ya, yb, face_x, face_y, scale):
    nx, ny, count, deep = cols.shape
    halo = Halo(odd, (xa, xb, ya, yb))
    for x in range(nx):
        scale[x] = inverse_diagonal(diag, halo, count, x)
    value = functools.partial(full_value, cols, inner, coeff, halo)
    for y in range(ny):
        face_x[pl.ds(y * count, count), :] = value(0, y) * row(scale, 0, y)
    face_x[pl.ds(ny * count, ny), :] = scale[0] * rhs[0]

    def side(y):
        for x in range(nx):
            face_y[pl.ds(x * count, count), :] = value(x, y) * row(scale, x, y)
            face_y[pl.ds(nx * count + x, 1), :] = row(scale, x, y) * row(rhs, x, y)

    @pl.when(odd[0] == 0)
    def _():
        side(0)

    @pl.when(odd[0] == 1)
    def _():
        side(ny - 1)


def border(odd, cols, inner, coeff, diag, rhs, halo):
    nx, ny, count, deep = cols.shape
    outs = (shape(ny * count + ny, deep), shape(nx * count + nx, deep))
    return call(
        border_kernel, outs, [SM] + [VM] * 9, [pltpu.VMEM((nx, ny, deep), F32)], limit=10
    )(odd, cols, inner, coeff, diag, rhs, *halo)


def local_kernel(
    odd, cols, inner, basis_stack, coeff, diag, rhs, xa, xb, ya, yb,
    part, scaled_stack, value_stack, pair_stack, scaled, scale, upper, scaled_rhs,
):
    nx, ny, count, deep = cols.shape
    halo = Halo(odd, (xa, xb, ya, yb))
    lane = lax.broadcasted_iota(jnp.int32, (ny, deep), 1)
    for x in range(nx):
        inverse = inverse_diagonal(diag, halo, count, x)
        scale[x] = inverse
        scaled_rhs[x] = inverse * rhs[x]
        upper[x] = jnp.where(lane == deep - 1, 0.0, coeff[2, x])
    for x in range(nx):
        for y in range(ny):
            value = full_value(cols, inner, coeff, halo, x, y)
            result = value * row(scale, x, y)
            scaled[x, y] = result
            put(value_stack, x * ny + y, value, row(rhs, x, y))
            put(scaled_stack, x * ny + y, result, row(scaled_rhs, x, y))
    for x in range(nx):
        for y in range(ny):
            over, ahead = row(upper, x, y), pltpu.roll(scaled[x, y], deep - 1, 1)
            pair = over * ahead
            pair_rhs = over * pltpu.roll(jnp.broadcast_to(row(scaled_rhs, x, y), (8, deep)), deep - 1, 1)[:1]
            if x + 1 < nx:
                pair += row(coeff, 0, x, y) * scaled[x + 1, y]
                pair_rhs += row(coeff, 0, x, y) * row(scaled_rhs, x + 1, y)
            if y + 1 < ny:
                pair += row(coeff, 1, x, y) * scaled[x, y + 1]
                pair_rhs += row(coeff, 1, x, y) * row(scaled_rhs, x, y + 1)
            put(pair_stack, x * ny + y, pair, pair_rhs)
    gram, projected = fold(by_rows(basis_stack[...], value_stack[...]), count)
    square, square_rhs = fold(by_rows(value_stack[...], scaled_stack[...]), count)
    pairs, pairs_rhs = fold(by_rows(scaled_stack[...], pair_stack[...]), count)
    part[...] = jnp.zeros_like(part)
    part[pl.ds(0, count), pl.ds(0, count)] = gram
    part[:, pl.ds(count, count)] = square
    part[:, pl.ds(2 * count, count)] = pairs
    part[pl.ds(0, count), pl.ds(3 * count, 1)] = projected
    part[:, pl.ds(3 * count + 1, 1)] = square_rhs
    part[:, pl.ds(3 * count + 2, 1)] = pairs_rhs


def local_sums(odd, cols, inner, basis_stack, coeff, diag, rhs, halo):
    nx, ny, count, deep = cols.shape
    cells = nx * ny * deep
    tall = 2 * count + EXTRA
    small = pltpu.VMEM((nx, ny, deep), F32)
    outs = (shape(count + 8, -(-(3 * count + 3) // LANES) * LANES), shape(tall, cells, dtype=BF16))
    return call(
        local_kernel,
        outs,
        [SM] + [VM] * 10,
        [
            pltpu.VMEM((tall, cells), BF16),
            pltpu.VMEM((tall, cells), BF16),
            pltpu.VMEM((nx, ny, count, deep), F32),
            small, small, small,
        ],
        limit=28,
        work=60 * count * cells,
        moved=24 * count * cells,
    )(odd, cols, inner, basis_stack, coeff, diag, rhs, *halo)


def shared_kernel(odd, part, scaled_stack, coeff, ya, yb, far_x, far_y, total, mine, pair_stack):
    halo = Halo(odd, (None, None, ya, yb))
    count = part.shape[0] - 8
    nx, ny, deep = coeff.shape[1:]
    for y in range(ny):
        face = row(coeff, 0, nx - 1, y)
        put(
            pair_stack, y, face * far_x[pl.ds(y * count, count), :],
            face * far_x[pl.ds(ny * count + y, 1), :],
        )
        mine[:, pl.ds(y * deep, deep)] = scaled_stack[:, pl.ds(((nx - 1) * ny + y) * deep, deep)]
    for x in range(nx):
        own = halo.rows(1, False, nx * count + x, 1)
        face = jnp.where(odd[0] == 0, row(coeff, 1, x, ny - 1), own)
        put(
            pair_stack, ny + x, face * far_y[pl.ds(x * count, count), :],
            face * far_y[pl.ds(nx * count + x, 1), :],
        )

    def side(y):
        for x in range(nx):
            mine[:, pl.ds((ny + x) * deep, deep)] = scaled_stack[:, pl.ds((x * ny + y) * deep, deep)]

    @pl.when(odd[0] == 0)
    def _():
        side(ny - 1)

    @pl.when(odd[0] == 1)
    def _():
        side(0)

    pairs, pairs_rhs = fold(by_rows(mine[...], pair_stack[...]), count)
    total[...] = part[...]
    total[:, pl.ds(2 * count, count)] += pairs
    total[:, pl.ds(3 * count + 2, 1)] += pairs_rhs


def shared_sums(odd, part, scaled_stack, coeff, ya, yb, far_x, far_y):
    nx, ny, deep = coeff.shape[1:]
    wide = pltpu.VMEM((scaled_stack.shape[0], (nx + ny) * deep), BF16)
    return call(
        shared_kernel, shape(*part.shape), [SM] + [VM] * 7, [wide, wide], limit=12
    )(odd, part, scaled_stack, coeff, ya, yb, far_x, far_y)


def finish_kernel(total, basis_stack, scaled_stack, guess, stepped):
    count = total.shape[0] - 8
    nx, ny, deep = guess.shape
    sums = total[pl.ds(0, count), :]
    work = sums
    level = lax.broadcasted_iota(jnp.int32, (count, 1), 0)
    for k in range(count):
        line = work[k : k + 1, :] / work[k : k + 1, k : k + 1]
        column = work[:, k : k + 1]
        work = jnp.where(level == k, line, work - column * line)
    at = 3 * count
    turned = work.T
    weights = work[:, at : at + 1]
    weights_row = turned[at : at + 1, :]
    shift_row = turned[at + 1 : at + 2, :] - jnp.sum(weights * turned[count : 2 * count, :], axis=0, keepdims=True)
    sums_row = sums.T
    rhs_row = sums_row[at + 1 : at + 2, :]
    both = jnp.sum(weights * sums, axis=0, keepdims=True)
    correction = rhs_row - both[:, count : 2 * count]
    along = jnp.sum(weights_row * (rhs_row + correction), axis=1, keepdims=True)
    tail = total[pl.ds(count, 1), :]
    size = tail[:, at + 1 : at + 2] - along
    crossing = jnp.sum(
        weights_row * (both[:, 2 * count : at] - sums_row[at + 2 : at + 3, :] - tail[:, 2 * count : at]),
        axis=1, keepdims=True,
    ) + tail[:, at + 2 : at + 3]
    lost = jnp.sum(correction * shift_row, axis=1, keepdims=True)
    step = size / (size - 2.0 * crossing - lost)
    first = lax.broadcasted_iota(jnp.int32, (EXTRA, count), 0)
    of_basis = jnp.where(first == 0, weights_row, jnp.where(first == 1, weights_row - step * shift_row, 0.0))
    of_scaled = jnp.where(first == 1, -step * weights_row, 0.0)
    last = lax.broadcasted_iota(jnp.int32, (EXTRA, EXTRA), 0)
    place = lax.broadcasted_iota(jnp.int32, (EXTRA, EXTRA), 1)
    of_rhs = jnp.where((last == 1) & (place < 2), step, 0.0)
    basis_high, basis_low = halves(jnp.concatenate([of_basis, of_basis], axis=1))
    scaled_high, scaled_low = halves(jnp.concatenate([of_scaled, of_scaled, of_rhs], axis=1))
    for x in range(nx):
        lanes = pl.ds(x * ny * deep, ny * deep)
        fields = basis_stack[:, lanes]
        result = jnp.dot(basis_high, fields, preferred_element_type=F32)
        result += jnp.dot(basis_low, fields, preferred_element_type=F32)
        fields = scaled_stack[:, lanes]
        result += jnp.dot(scaled_high, fields, preferred_element_type=F32)
        result += jnp.dot(scaled_low, fields, preferred_element_type=F32)
        for y in range(ny):
            guess[x, pl.ds(y, 1), :] = result[0:1, y * deep : (y + 1) * deep]
            stepped[x, pl.ds(y, 1), :] = result[1:2, y * deep : (y + 1) * deep]


def finish(total, basis_stack, scaled_stack, block):
    return call(finish_kernel, (shape(*block),) * 2, [VM] * 3, limit=24)(
        total, basis_stack, scaled_stack
    )


def on_device(basis, rhs, extra_diag, coeff):
    odd = jnp.stack([lax.axis_index("gx") % 2, lax.axis_index("gy") % 2]).astype(jnp.int32)
    first_x, second_x, first_y, second_y = faces(odd, basis, coeff)
    first_y, second_y = swap(first_y, "gy", 0), swap(second_y, "gy", 1)
    first_x, second_x = swap(first_x, "gx", 0), swap(second_x, "gx", 1)
    cols, inner, basis_stack, diag = inside(basis, coeff, extra_diag)
    halo = (first_x, second_x, first_y, second_y)
    face_x, face_y = border(odd, cols, inner, coeff, diag, rhs, halo)
    wide, deep = lax.axis_size("gx"), lax.axis_size("gy")
    route = []
    for i in range(wide):
        step = 1 if i % 2 else -1
        route += [(i * deep + j, i * deep + j + step) for j in range(deep) if 0 <= j + step < deep]
    far_y = lax.ppermute(face_y, ("gx", "gy"), route)
    far_x = send(face_x, "gx", -1)
    part, scaled_stack = local_sums(odd, cols, inner, basis_stack, coeff, diag, rhs, halo)
    part = shared_sums(odd, part, scaled_stack, coeff, first_y, second_y, far_x, far_y)
    total = sum_all(part)
    return finish(total, basis_stack, scaled_stack, rhs.shape)


def solution(mesh):
    placed = (
        P(None, "gx", "gy", None),
        P("gx", "gy", None),
        P("gx", "gy", None),
        P(None, "gx", "gy", None),
    )
    return jax.shard_map(
        on_device,
        mesh=mesh,
        in_specs=placed,
        out_specs=(P("gx", "gy", None), P("gx", "gy", None)),
        check_vma=False,
    )
```

```python
import functools
import jax
import jax.numpy as jnp
from jax import lax
from jax.experimental import pallas as pl
from jax.experimental.pallas import tpu as pltpu
from jax.sharding import PartitionSpec as P

F32 = jnp.float32
BF16 = jnp.bfloat16
EXTRA = 16
LANES = 128
VM = pl.BlockSpec(memory_space=pltpu.VMEM)
RAW = pl.BlockSpec(memory_space=pl.ANY)


def shape(*dims, dtype=F32):
    return jax.ShapeDtypeStruct(dims, dtype)


def call(body, outs, ins, scratch=(), limit=24, work=0, moved=0):
    return pl.pallas_call(
        body,
        out_shape=outs,
        in_specs=ins,
        out_specs=jax.tree.map(lambda _: VM, outs),
        scratch_shapes=list(scratch),
        compiler_params=pltpu.CompilerParams(vmem_limit_bytes=limit << 20),
        cost_estimate=pl.CostEstimate(flops=work, bytes_accessed=moved, transcendentals=0),
    )


def sum_stages():
    wide, deep = lax.axis_size("gx"), lax.axis_size("gy")
    along_x = [(1 << k, 0) for k in range(wide.bit_length() - 1)]
    along_y = [(0, 1 << k) for k in range(deep.bit_length() - 1)]
    steps = along_y[:0:-1] + along_x + along_y[:1]
    single = len(steps) % 2
    stages = [[step] for step in steps[:single]]
    for at in range(single, len(steps), 2):
        (a, b), (c, d) = steps[at], steps[at + 1]
        stages.append([(a, b), (c, d), (a ^ c, b ^ d)])
    return stages


def sum_all(part):
    wide, deep = lax.axis_size("gx"), lax.axis_size("gy")
    if wide & (wide - 1) or deep & (deep - 1):
        return lax.psum(part, ("gx", "gy"))
    devices = [(i, j) for i in range(wide) for j in range(deep)]
    for stage in sum_stages():
        others = [
            lax.ppermute(
                part,
                ("gx", "gy"),
                [(i * deep + j, (i ^ a) * deep + (j ^ b)) for i, j in devices],
            )
            for a, b in stage
        ]
        for other in others:
            part = part + other
    return part


def send(block, axis, step):
    size = lax.axis_size(axis)
    return lax.ppermute(block, axis, [(i, i + step) for i in range(size) if 0 <= i + step < size])


def swap(block, axis, start):
    size = lax.axis_size(axis)
    pairs = [(i, i + 1) for i in range(start, size - 1, 2)]
    return lax.ppermute(block, axis, pairs + [(j, i) for i, j in pairs])


def halves(value):
    high = value.astype(BF16)
    return high, (value - high.astype(F32)).astype(BF16)


def put(stack, at, value, extra=None):
    count, deep = value.shape
    lanes = pl.ds(at * deep if isinstance(at, int) else pl.multiple_of(at * deep, deep), deep)
    high, low = halves(value)
    stack[pl.ds(0, count), lanes] = high
    stack[pl.ds(count, count), lanes] = low
    if extra is not None:
        high, low = halves(extra)
        row = lax.broadcasted_iota(jnp.int32, (EXTRA, deep), 0)
        both = jnp.where(row == 0, high.astype(F32), jnp.where(row == 1, low.astype(F32), 0.0))
        stack[pl.ds(2 * count, EXTRA), lanes] = both.astype(BF16)


def by_rows(left, right):
    return lax.dot_general(left, right, (((1,), (1,)), ((), ())), preferred_element_type=F32)


def fold_rows(full, count):
    top = full[:count] + full[count : 2 * count]
    if full.shape[0] == 2 * count:
        return top
    last = full[2 * count : 2 * count + 1] + full[2 * count + 1 : 2 * count + 2]
    return jnp.concatenate([top, jnp.broadcast_to(last, (8, full.shape[1]))], axis=0)


def fold(full, count):
    rows = fold_rows(full, count)
    body = rows[:, :count] + rows[:, count : 2 * count]
    last = rows[:, 2 * count : 2 * count + 1] + rows[:, 2 * count + 1 : 2 * count + 2]
    return body, last


def parity():
    return lax.axis_index("gx") % 2, lax.axis_index("gy") % 2


def faces_kernel(basis, coeff, first_x, second_x, first_y, second_y, cols, slabs, sems):
    count, nx, ny, deep = basis.shape
    odd = parity()
    copies = [pltpu.make_async_copy(basis.at[:, x], slabs.at[x], sems.at[x]) for x in range(nx)]
    ends = []
    for k, target in enumerate((first_x, second_x)):
        ends.append((coeff.at[0, nx - 1], target.at[pl.ds(ny * count, ny)]))
    for k, target in enumerate((first_y, second_y)):
        ends.append((coeff.at[1, :, ny - 1, :], target.at[pl.ds(nx * count, nx)]))
    ends = [pltpu.make_async_copy(a, b, sems.at[nx + k]) for k, (a, b) in enumerate(ends)]
    for copy in copies + ends:
        copy.start()
    for x in range(nx):
        copies[x].wait()
        slab = jnp.swapaxes(slabs[x], 0, 1)
        cols[x] = slab
        rows = pl.ds(x * count, count)
        first_y[rows, :] = jnp.where(odd[1] == 0, slab[ny - 1], slab[0])
        second_y[rows, :] = jnp.where(odd[1] == 0, slab[0], slab[ny - 1])
    for y in range(ny):
        rows = pl.ds(y * count, count)
        first_x[rows, :] = jnp.where(odd[0] == 0, cols[nx - 1, y], cols[0, y])
        second_x[rows, :] = jnp.where(odd[0] == 0, cols[0, y], cols[nx - 1, y])
    for copy in ends:
        copy.wait()


def faces(basis, coeff):
    count, nx, ny, deep = basis.shape
    of_x, of_y = shape(ny * count + ny, deep), shape(nx * count + nx, deep)
    outs = (of_x, of_x, of_y, of_y, shape(nx, ny, count, deep))
    slabs = pltpu.VMEM((nx, count, ny, deep), F32)
    sems = pltpu.SemaphoreType.DMA((nx + 4,))
    return call(faces_kernel, outs, [RAW, RAW], [slabs, sems], limit=40)(basis, coeff)


def row(ref, *at):
    return ref[at[:-1] + (pl.ds(at[-1], 1), slice(None))]


def near_z(field, upper, lower):
    deep = field.shape[1]
    above, below = pltpu.roll(field, deep - 1, 1), pltpu.roll(field, 1, 1)
    return upper * above + lower * below


def inner_kernel(cols, coeff, extra_raw, inner, stack, diag, upper, lower, ahead, behind, extra, sem):
    nx, ny, count, deep = cols.shape
    extra_copy = pltpu.make_async_copy(extra_raw, extra, sem)
    extra_copy.start()
    level = lax.broadcasted_iota(jnp.int32, (ny, deep), 0)
    lane = lax.broadcasted_iota(jnp.int32, (ny, deep), 1)
    extra_copy.wait()
    for x in range(nx):
        cx, cy, cz = coeff[0, x], coeff[1, x], coeff[2, x]
        upper[x] = jnp.where(lane == deep - 1, 0.0, cz)
        under = jnp.where(lane == 0, 0.0, pltpu.roll(cz, 1, 1))
        lower[x] = under
        before = coeff[0, x - 1] if x else jnp.zeros_like(cx)
        behind[x] = before
        ahead[x] = cx if x + 1 < nx else jnp.zeros_like(cx)
        total = extra[x] + cx + cy + cz + under + before
        diag[x] = total + jnp.where(level == 0, 0.0, pltpu.roll(cy, 1, 0))

    def slab(x, carry):
        after, before = jnp.minimum(x + 1, nx - 1), jnp.maximum(x - 1, 0)
        for y in range(ny):
            here = cols[x, y]
            sums = near_z(here, row(upper, x, y), row(lower, x, y))
            sums += row(ahead, x, y) * cols[after, y]
            sums += row(behind, x, y) * cols[before, y]
            if y + 1 < ny:
                sums += row(coeff, 1, x, y) * cols[x, y + 1]
            if y:
                sums += row(coeff, 1, x, y - 1) * cols[x, y - 1]
            inner[x, y] = row(diag, x, y) * here - sums
            put(stack, x * ny + y, here)
        return carry

    lax.fori_loop(0, nx, slab, 0)


def inside(cols, coeff, extra):
    nx, ny, count, deep = cols.shape
    cells = nx * ny * deep
    outs = (shape(nx, ny, count, deep), shape(2 * count, cells, dtype=BF16), shape(nx, ny, deep))
    small = pltpu.VMEM((nx, ny, deep), F32)
    return call(
        inner_kernel, outs, [VM, VM, RAW], [small] * 5 + [pltpu.SemaphoreType.DMA],
        work=20 * count * cells, moved=16 * count * cells,
    )(cols, coeff, extra)


class Halo:
    def __init__(self, odd, refs):
        self.odd = odd
        self.refs = refs

    def rows(self, axis, upper, start, size):
        first, second = self.refs[2 * axis : 2 * axis + 2]
        here = pl.ds(start, size)
        return jnp.where(self.odd[axis] == (0 if upper else 1), first[here, :], second[here, :])


def inverse_diagonal(diag, halo, count, x):
    nx, ny, deep = diag.shape
    level = lax.broadcasted_iota(jnp.int32, (ny, deep), 0)
    total = diag[x] + jnp.where(level == 0, halo.rows(1, False, nx * count + x, 1), 0.0)
    if x == 0:
        total += halo.rows(0, False, ny * count, ny)
    return 1.0 / total


def full_value(cols, inner, coeff, halo, x, y):
    nx, ny, count, deep = cols.shape
    value = inner[x, y]
    if x == 0:
        value += halo.rows(0, False, ny * count + y, 1) * (cols[x, y] - halo.rows(0, False, y * count, count))
    if x == nx - 1:
        value -= row(coeff, 0, x, y) * halo.rows(0, True, y * count, count)
    if y == 0:
        value += halo.rows(1, False, nx * count + x, 1) * (cols[x, y] - halo.rows(1, False, x * count, count))
    if y == ny - 1:
        value -= row(coeff, 1, x, y) * halo.rows(1, True, x * count, count)
    return value


def border_kernel(cols, inner, coeff, diag, rhs, xa, xb, ya, yb, face_x, face_y, scale):
    nx, ny, count, deep = cols.shape
    odd = parity()
    halo = Halo(odd, (xa, xb, ya, yb))
    for x in range(nx):
        scale[x] = inverse_diagonal(diag, halo, count, x)
    value = functools.partial(full_value, cols, inner, coeff, halo)
    for y in range(ny):
        face_x[pl.ds(y * count, count), :] = value(0, y) * row(scale, 0, y)
    face_x[pl.ds(ny * count, ny), :] = scale[0] * rhs[0]

    def side(y):
        for x in range(nx):
            face_y[pl.ds(x * count, count), :] = value(x, y) * row(scale, x, y)
            face_y[pl.ds(nx * count + x, 1), :] = row(scale, x, y) * row(rhs, x, y)

    @pl.when(odd[0] == 0)
    def _():
        side(0)

    @pl.when(odd[0] == 1)
    def _():
        side(ny - 1)


def border(cols, inner, coeff, diag, rhs, halo):
    nx, ny, count, deep = cols.shape
    outs = (shape(ny * count + ny, deep), shape(nx * count + nx, deep))
    return call(
        border_kernel, outs, [VM] * 9, [pltpu.VMEM((nx, ny, deep), F32)], limit=10
    )(cols, inner, coeff, diag, rhs, *halo)


def local_kernel(
    cols, inner, basis_stack, coeff, diag, rhs, xa, xb, ya, yb,
    part, scaled_stack, value_stack, pair_stack, scaled, scale, upper, scaled_rhs,
):
    nx, ny, count, deep = cols.shape
    odd = parity()
    halo = Halo(odd, (xa, xb, ya, yb))
    lane = lax.broadcasted_iota(jnp.int32, (ny, deep), 1)
    for x in range(nx):
        inverse = inverse_diagonal(diag, halo, count, x)
        scale[x] = inverse
        scaled_rhs[x] = inverse * rhs[x]
        upper[x] = jnp.where(lane == deep - 1, 0.0, coeff[2, x])
    for x in range(nx):
        for y in range(ny):
            value = full_value(cols, inner, coeff, halo, x, y)
            result = value * row(scale, x, y)
            scaled[x, y] = result
            put(value_stack, x * ny + y, value, row(rhs, x, y))
            put(scaled_stack, x * ny + y, result, row(scaled_rhs, x, y))
    for x in range(nx):
        for y in range(ny):
            over, ahead = row(upper, x, y), pltpu.roll(scaled[x, y], deep - 1, 1)
            pair = over * ahead
            pair_rhs = over * pltpu.roll(jnp.broadcast_to(row(scaled_rhs, x, y), (8, deep)), deep - 1, 1)[:1]
            if x + 1 < nx:
                pair += row(coeff, 0, x, y) * scaled[x + 1, y]
                pair_rhs += row(coeff, 0, x, y) * row(scaled_rhs, x + 1, y)
            if y + 1 < ny:
                pair += row(coeff, 1, x, y) * scaled[x, y + 1]
                pair_rhs += row(coeff, 1, x, y) * row(scaled_rhs, x, y + 1)
            put(pair_stack, x * ny + y, pair, pair_rhs)
    gram, projected = fold(by_rows(basis_stack[...], value_stack[...]), count)
    square, square_rhs = fold(by_rows(value_stack[...], scaled_stack[...]), count)
    pairs, pairs_rhs = fold(by_rows(scaled_stack[...], pair_stack[...]), count)
    part[...] = jnp.zeros_like(part)
    part[pl.ds(0, count), pl.ds(0, count)] = gram
    part[:, pl.ds(count, count)] = square
    part[:, pl.ds(2 * count, count)] = pairs
    part[pl.ds(0, count), pl.ds(3 * count, 1)] = projected
    part[:, pl.ds(3 * count + 1, 1)] = square_rhs
    part[:, pl.ds(3 * count + 2, 1)] = pairs_rhs


def local_sums(cols, inner, basis_stack, coeff, diag, rhs, halo):
    nx, ny, count, deep = cols.shape
    cells = nx * ny * deep
    tall = 2 * count + EXTRA
    small = pltpu.VMEM((nx, ny, deep), F32)
    outs = (shape(count + 8, -(-(3 * count + 3) // LANES) * LANES), shape(tall, cells, dtype=BF16))
    return call(
        local_kernel,
        outs,
        [VM] * 10,
        [
            pltpu.VMEM((tall, cells), BF16),
            pltpu.VMEM((tall, cells), BF16),
            pltpu.VMEM((nx, ny, count, deep), F32),
            small, small, small,
        ],
        limit=28,
        work=60 * count * cells,
        moved=24 * count * cells,
    )(cols, inner, basis_stack, coeff, diag, rhs, *halo)


def shared_kernel(part, scaled_stack, coeff, ya, yb, far_x, far_y, total, mine, pair_stack):
    odd = parity()
    halo = Halo(odd, (None, None, ya, yb))
    count = part.shape[0] - 8
    nx, ny, deep = coeff.shape[1:]
    for y in range(ny):
        face = row(coeff, 0, nx - 1, y)
        put(
            pair_stack, y, face * far_x[pl.ds(y * count, count), :],
            face * far_x[pl.ds(ny * count + y, 1), :],
        )
        mine[:, pl.ds(y * deep, deep)] = scaled_stack[:, pl.ds(((nx - 1) * ny + y) * deep, deep)]
    for x in range(nx):
        own = halo.rows(1, False, nx * count + x, 1)
        face = jnp.where(odd[0] == 0, row(coeff, 1, x, ny - 1), own)
        put(
            pair_stack, ny + x, face * far_y[pl.ds(x * count, count), :],
            face * far_y[pl.ds(nx * count + x, 1), :],
        )

    def side(y):
        for x in range(nx):
            mine[:, pl.ds((ny + x) * deep, deep)] = scaled_stack[:, pl.ds((x * ny + y) * deep, deep)]

    @pl.when(odd[0] == 0)
    def _():
        side(ny - 1)

    @pl.when(odd[0] == 1)
    def _():
        side(0)

    pairs, pairs_rhs = fold(by_rows(mine[...], pair_stack[...]), count)
    total[...] = part[...]
    total[:, pl.ds(2 * count, count)] += pairs
    total[:, pl.ds(3 * count + 2, 1)] += pairs_rhs


def shared_sums(part, scaled_stack, coeff, ya, yb, far_x, far_y):
    nx, ny, deep = coeff.shape[1:]
    wide = pltpu.VMEM((scaled_stack.shape[0], (nx + ny) * deep), BF16)
    return call(
        shared_kernel, shape(*part.shape), [VM] * 7, [wide, wide], limit=12
    )(part, scaled_stack, coeff, ya, yb, far_x, far_y)


def inverse_two(a, b, c, d):
    scale = 1.0 / (a * d - b * c)
    return d * scale, -b * scale, -c * scale, a * scale


def apply_two(matrix, first, second):
    a, b, c, d = matrix
    return a * first + b * second, c * first + d * second


def finish_kernel(total, basis_stack, scaled_stack, guess, stepped):
    count = total.shape[0] - 8
    nx, ny, deep = guess.shape
    sums = total[pl.ds(0, count), :]
    level = lax.broadcasted_iota(jnp.int32, (count, 1), 0)
    lane = lax.broadcasted_iota(jnp.int32, sums.shape, 1)
    own = jnp.where(lane == level, sums, 0.0)
    of_row = lax.rsqrt(jnp.sum(own, axis=1, keepdims=True))
    of_lane = lax.rsqrt(jnp.sum(own, axis=0, keepdims=True))
    work = sums * of_row * jnp.where(lane[:1] < count, of_lane, 1.0)
    for k in range(0, count, 4):
        columns = [jnp.broadcast_to(work[:, k + b : k + b + 1], work.shape) for b in range(4)]
        rows = [work[k + a : k + a + 1, :] for a in range(4)]
        pivot = [[column[k + a : k + a + 1, :] for column in columns] for a in range(4)]
        top = inverse_two(pivot[0][0], pivot[0][1], pivot[1][0], pivot[1][1])
        line_0, line_1 = apply_two(top, rows[0], rows[1])
        across = [apply_two(top, pivot[0][b], pivot[1][b]) for b in (2, 3)]
        low = [rows[a] - pivot[a][0] * line_0 - pivot[a][1] * line_1 for a in (2, 3)]
        rest = [
            [pivot[a][b] - pivot[a][0] * across[b - 2][0] - pivot[a][1] * across[b - 2][1] for b in (2, 3)]
            for a in (2, 3)
        ]
        line_2, line_3 = apply_two(inverse_two(*rest[0], *rest[1]), *low)
        line_0 = line_0 - across[0][0] * line_2 - across[1][0] * line_3
        line_1 = line_1 - across[0][1] * line_2 - across[1][1] * line_3
        lines = (line_0, line_1, line_2, line_3)
        for a in range(4):
            work = work - columns[a] * lines[a]
        for a in range(4):
            work = jnp.where(level == k + a, lines[a], work)
    at = 3 * count
    work = work * of_row
    turned = work.T
    weights = work[:, at : at + 1]
    weights_row = turned[at : at + 1, :]
    shift_row = turned[at + 1 : at + 2, :] - jnp.sum(weights * turned[count : 2 * count, :], axis=0, keepdims=True)
    sums_row = sums.T
    rhs_row = sums_row[at + 1 : at + 2, :]
    both = jnp.sum(weights * sums, axis=0, keepdims=True)
    correction = rhs_row - both[:, count : 2 * count]
    along = jnp.sum(weights_row * (rhs_row + correction), axis=1, keepdims=True)
    tail = total[pl.ds(count, 1), :]
    size = tail[:, at + 1 : at + 2] - along
    crossing = jnp.sum(
        weights_row * (both[:, 2 * count : at] - sums_row[at + 2 : at + 3, :] - tail[:, 2 * count : at]),
        axis=1, keepdims=True,
    ) + tail[:, at + 2 : at + 3]
    lost = jnp.sum(correction * shift_row, axis=1, keepdims=True)
    step = size / (size - 2.0 * crossing - lost)
    first = lax.broadcasted_iota(jnp.int32, (EXTRA, count), 0)
    of_basis = jnp.where(first == 0, weights_row, jnp.where(first == 1, weights_row - step * shift_row, 0.0))
    of_scaled = jnp.where(first == 1, -step * weights_row, 0.0)
    last = lax.broadcasted_iota(jnp.int32, (EXTRA, EXTRA), 0)
    place = lax.broadcasted_iota(jnp.int32, (EXTRA, EXTRA), 1)
    of_rhs = jnp.where((last == 1) & (place < 2), step, 0.0)
    basis_high, basis_low = halves(jnp.concatenate([of_basis, of_basis], axis=1))
    scaled_high, scaled_low = halves(jnp.concatenate([of_scaled, of_scaled, of_rhs], axis=1))
    for x in range(nx):
        lanes = pl.ds(x * ny * deep, ny * deep)
        fields = basis_stack[:, lanes]
        result = jnp.dot(basis_high, fields, preferred_element_type=F32)
        result += jnp.dot(basis_low, fields, preferred_element_type=F32)
        fields = scaled_stack[:, lanes]
        result += jnp.dot(scaled_high, fields, preferred_element_type=F32)
        result += jnp.dot(scaled_low, fields, preferred_element_type=F32)
        for y in range(ny):
            guess[x, pl.ds(y, 1), :] = result[0:1, y * deep : (y + 1) * deep]
            stepped[x, pl.ds(y, 1), :] = result[1:2, y * deep : (y + 1) * deep]


def finish(total, basis_stack, scaled_stack, block):
    return call(finish_kernel, (shape(*block),) * 2, [VM] * 3, limit=24)(
        total, basis_stack, scaled_stack
    )


def on_device(basis, rhs, extra_diag, coeff):
    first_x, second_x, first_y, second_y, cols = faces(basis, coeff)
    first_y, second_y = swap(first_y, "gy", 0), swap(second_y, "gy", 1)
    first_x, second_x = swap(first_x, "gx", 0), swap(second_x, "gx", 1)
    inner, basis_stack, diag = inside(cols, coeff, extra_diag)
    halo = (first_x, second_x, first_y, second_y)
    face_x, face_y = border(cols, inner, coeff, diag, rhs, halo)
    wide, deep = lax.axis_size("gx"), lax.axis_size("gy")
    route = []
    for i in range(wide):
        step = 1 if i % 2 else -1
        route += [(i * deep + j, i * deep + j + step) for j in range(deep) if 0 <= j + step < deep]
    far_y = lax.ppermute(face_y, ("gx", "gy"), route)
    far_x = send(face_x, "gx", -1)
    part, scaled_stack = local_sums(cols, inner, basis_stack, coeff, diag, rhs, halo)
    part = shared_sums(part, scaled_stack, coeff, first_y, second_y, far_x, far_y)
    total = sum_all(part)
    return finish(total, basis_stack, scaled_stack, rhs.shape)


def solution(mesh):
    placed = (
        P(None, "gx", "gy", None),
        P("gx", "gy", None),
        P("gx", "gy", None),
        P(None, "gx", "gy", None),
    )
    return jax.shard_map(
        on_device,
        mesh=mesh,
        in_specs=placed,
        out_specs=(P("gx", "gy", None), P("gx", "gy", None)),
        check_vma=False,
    )
```

```python
import functools
import jax
import jax.numpy as jnp
from jax import lax
from jax.experimental import pallas as pl
from jax.experimental.pallas import tpu as pltpu
from jax.sharding import PartitionSpec as P

F32 = jnp.float32
BF16 = jnp.bfloat16
EXTRA = 16
LANES = 128
VM = pl.BlockSpec(memory_space=pltpu.VMEM)
RAW = pl.BlockSpec(memory_space=pl.ANY)


def shape(*dims, dtype=F32):
    return jax.ShapeDtypeStruct(dims, dtype)


def call(body, outs, ins, scratch=(), limit=24, work=0, moved=0):
    return pl.pallas_call(
        body,
        out_shape=outs,
        in_specs=ins,
        out_specs=jax.tree.map(lambda _: VM, outs),
        scratch_shapes=list(scratch),
        compiler_params=pltpu.CompilerParams(vmem_limit_bytes=limit << 20),
        cost_estimate=pl.CostEstimate(flops=work, bytes_accessed=moved, transcendentals=0),
    )


def sum_stages():
    wide, deep = lax.axis_size("gx"), lax.axis_size("gy")
    along_x = [(1 << k, 0) for k in range(wide.bit_length() - 1)]
    along_y = [(0, 1 << k) for k in range(deep.bit_length() - 1)]
    steps = along_y[:0:-1] + along_x + along_y[:1]
    single = len(steps) % 2
    stages = [[step] for step in steps[:single]]
    for at in range(single, len(steps), 2):
        (a, b), (c, d) = steps[at], steps[at + 1]
        stages.append([(a, b), (c, d), (a ^ c, b ^ d)])
    return stages


def sum_all(part):
    wide, deep = lax.axis_size("gx"), lax.axis_size("gy")
    if wide & (wide - 1) or deep & (deep - 1):
        return lax.psum(part, ("gx", "gy"))
    devices = [(i, j) for i in range(wide) for j in range(deep)]
    for stage in sum_stages():
        others = [
            lax.ppermute(
                part,
                ("gx", "gy"),
                [(i * deep + j, (i ^ a) * deep + (j ^ b)) for i, j in devices],
            )
            for a, b in stage
        ]
        for other in others:
            part = part + other
    return part


def send(block, axis, step):
    size = lax.axis_size(axis)
    return lax.ppermute(block, axis, [(i, i + step) for i in range(size) if 0 <= i + step < size])


def swap(block, axis, start):
    size = lax.axis_size(axis)
    pairs = [(i, i + 1) for i in range(start, size - 1, 2)]
    return lax.ppermute(block, axis, pairs + [(j, i) for i, j in pairs])


def halves(value):
    high = value.astype(BF16)
    return high, (value - high.astype(F32)).astype(BF16)


def put(stack, at, value, extra=None):
    count, deep = value.shape
    lanes = pl.ds(at * deep if isinstance(at, int) else pl.multiple_of(at * deep, deep), deep)
    high, low = halves(value)
    stack[pl.ds(0, count), lanes] = high
    stack[pl.ds(count, count), lanes] = low
    if extra is not None:
        high, low = halves(extra)
        row = lax.broadcasted_iota(jnp.int32, (EXTRA, deep), 0)
        both = jnp.where(row == 0, high.astype(F32), jnp.where(row == 1, low.astype(F32), 0.0))
        stack[pl.ds(2 * count, EXTRA), lanes] = both.astype(BF16)


def by_rows(left, right):
    return lax.dot_general(left, right, (((1,), (1,)), ((), ())), preferred_element_type=F32)


def fold_rows(full, count):
    top = full[:count] + full[count : 2 * count]
    if full.shape[0] == 2 * count:
        return top
    last = full[2 * count : 2 * count + 1] + full[2 * count + 1 : 2 * count + 2]
    return jnp.concatenate([top, jnp.broadcast_to(last, (8, full.shape[1]))], axis=0)


def fold(full, count):
    rows = fold_rows(full, count)
    body = rows[:, :count] + rows[:, count : 2 * count]
    last = rows[:, 2 * count : 2 * count + 1] + rows[:, 2 * count + 1 : 2 * count + 2]
    return body, last


def parity():
    return lax.axis_index("gx") % 2, lax.axis_index("gy") % 2


def faces_kernel(basis, coeff, first_x, second_x, first_y, second_y, cols, slabs, sems):
    count, nx, ny, _ = basis.shape
    odd = parity()
    copies = [pltpu.make_async_copy(basis.at[:, x], slabs.at[x], sems.at[x]) for x in range(nx)]
    ends = []
    for target in (first_x, second_x):
        ends.append((coeff.at[0, nx - 1], target.at[pl.ds(ny * count, ny)]))
    for target in (first_y, second_y):
        ends.append((coeff.at[1, :, ny - 1, :], target.at[pl.ds(nx * count, nx)]))
    ends = [pltpu.make_async_copy(a, b, sems.at[nx + k]) for k, (a, b) in enumerate(ends)]
    for copy in copies + ends:
        copy.start()
    for x in range(nx):
        copies[x].wait()
        slab = jnp.swapaxes(slabs[x], 0, 1)
        cols[x] = slab
        rows = pl.ds(x * count, count)
        first_y[rows, :] = jnp.where(odd[1] == 0, slab[ny - 1], slab[0])
        second_y[rows, :] = jnp.where(odd[1] == 0, slab[0], slab[ny - 1])
    for y in range(ny):
        rows = pl.ds(y * count, count)
        first_x[rows, :] = jnp.where(odd[0] == 0, cols[nx - 1, y], cols[0, y])
        second_x[rows, :] = jnp.where(odd[0] == 0, cols[0, y], cols[nx - 1, y])
    for copy in ends:
        copy.wait()


def faces(basis, coeff):
    count, nx, ny, deep = basis.shape
    of_x, of_y = shape(ny * count + ny, deep), shape(nx * count + nx, deep)
    outs = (of_x, of_x, of_y, of_y, shape(nx, ny, count, deep))
    slabs = pltpu.VMEM((nx, count, ny, deep), F32)
    sems = pltpu.SemaphoreType.DMA((nx + 4,))
    return call(faces_kernel, outs, [RAW, RAW], [slabs, sems], limit=50)(basis, coeff)


def row(ref, *at):
    return ref[at[:-1] + (pl.ds(at[-1], 1), slice(None))]


def near_z(field, upper, lower):
    deep = field.shape[1]
    above, below = pltpu.roll(field, deep - 1, 1), pltpu.roll(field, 1, 1)
    return upper * above + lower * below


def inner_kernel(cols, coeff, extra_raw, inner, stack, diag, upper, lower, ahead, behind, extra, sem):
    nx, ny, _, deep = cols.shape
    extra_copy = pltpu.make_async_copy(extra_raw, extra, sem)
    extra_copy.start()
    level = lax.broadcasted_iota(jnp.int32, (ny, deep), 0)
    lane = lax.broadcasted_iota(jnp.int32, (ny, deep), 1)
    extra_copy.wait()
    for x in range(nx):
        cx, cy, cz = coeff[0, x], coeff[1, x], coeff[2, x]
        upper[x] = jnp.where(lane == deep - 1, 0.0, cz)
        under = jnp.where(lane == 0, 0.0, pltpu.roll(cz, 1, 1))
        lower[x] = under
        before = coeff[0, x - 1] if x else jnp.zeros_like(cx)
        behind[x] = before
        ahead[x] = cx if x + 1 < nx else jnp.zeros_like(cx)
        total = extra[x] + cx + cy + cz + under + before
        diag[x] = total + jnp.where(level == 0, 0.0, pltpu.roll(cy, 1, 0))

    def slab(x, carry):
        after, before = jnp.minimum(x + 1, nx - 1), jnp.maximum(x - 1, 0)
        for y in range(ny):
            here = cols[x, y]
            sums = near_z(here, row(upper, x, y), row(lower, x, y))
            sums += row(ahead, x, y) * cols[after, y]
            sums += row(behind, x, y) * cols[before, y]
            if y + 1 < ny:
                sums += row(coeff, 1, x, y) * cols[x, y + 1]
            if y:
                sums += row(coeff, 1, x, y - 1) * cols[x, y - 1]
            inner[x, y] = row(diag, x, y) * here - sums
            put(stack, x * ny + y, here)
        return carry

    lax.fori_loop(0, nx, slab, 0)


def inside(cols, coeff, extra):
    nx, ny, count, deep = cols.shape
    cells = nx * ny * deep
    outs = (shape(nx, ny, count, deep), shape(2 * count, cells, dtype=BF16), shape(nx, ny, deep))
    small = pltpu.VMEM((nx, ny, deep), F32)
    return call(
        inner_kernel, outs, [VM, VM, RAW], [small] * 5 + [pltpu.SemaphoreType.DMA],
        work=20 * count * cells, moved=16 * count * cells,
    )(cols, coeff, extra)


class Halo:
    def __init__(self, odd, refs):
        self.odd = odd
        self.refs = refs

    def rows(self, axis, upper, start, size):
        first, second = self.refs[2 * axis : 2 * axis + 2]
        here = pl.ds(start, size)
        return jnp.where(self.odd[axis] == (0 if upper else 1), first[here, :], second[here, :])


def inverse_diagonal(diag, halo, count, x):
    nx, ny, deep = diag.shape
    level = lax.broadcasted_iota(jnp.int32, (ny, deep), 0)
    total = diag[x] + jnp.where(level == 0, halo.rows(1, False, nx * count + x, 1), 0.0)
    if x == 0:
        total += halo.rows(0, False, ny * count, ny)
    return 1.0 / total


def full_value(cols, inner, coeff, halo, x, y):
    nx, ny, count, _ = cols.shape
    value = inner[x, y]
    if x == 0:
        value += halo.rows(0, False, ny * count + y, 1) * (cols[x, y] - halo.rows(0, False, y * count, count))
    if x == nx - 1:
        value -= row(coeff, 0, x, y) * halo.rows(0, True, y * count, count)
    if y == 0:
        value += halo.rows(1, False, nx * count + x, 1) * (cols[x, y] - halo.rows(1, False, x * count, count))
    if y == ny - 1:
        value -= row(coeff, 1, x, y) * halo.rows(1, True, x * count, count)
    return value


def border_kernel(cols, inner, coeff, diag, rhs, xa, xb, ya, yb, face_x, face_y, scale):
    nx, ny, count, _ = cols.shape
    odd = parity()
    halo = Halo(odd, (xa, xb, ya, yb))
    for x in range(nx):
        scale[x] = inverse_diagonal(diag, halo, count, x)
    value = functools.partial(full_value, cols, inner, coeff, halo)
    for y in range(ny):
        face_x[pl.ds(y * count, count), :] = value(0, y) * row(scale, 0, y)
    face_x[pl.ds(ny * count, ny), :] = scale[0] * rhs[0]

    def side(y):
        for x in range(nx):
            face_y[pl.ds(x * count, count), :] = value(x, y) * row(scale, x, y)
            face_y[pl.ds(nx * count + x, 1), :] = row(scale, x, y) * row(rhs, x, y)

    @pl.when(odd[0] == 0)
    def _():
        side(0)

    @pl.when(odd[0] == 1)
    def _():
        side(ny - 1)


def border(cols, inner, coeff, diag, rhs, halo):
    nx, ny, count, deep = cols.shape
    outs = (shape(ny * count + ny, deep), shape(nx * count + nx, deep))
    return call(
        border_kernel, outs, [VM] * 9, [pltpu.VMEM((nx, ny, deep), F32)], limit=10
    )(cols, inner, coeff, diag, rhs, *halo)


def local_kernel(
    cols, inner, basis_stack, coeff, diag, rhs, xa, xb, ya, yb,
    part, scaled_stack, value_stack, pair_stack, scaled, scale, upper, scaled_rhs,
):
    nx, ny, count, deep = cols.shape
    odd = parity()
    halo = Halo(odd, (xa, xb, ya, yb))
    lane = lax.broadcasted_iota(jnp.int32, (ny, deep), 1)
    for x in range(nx):
        inverse = inverse_diagonal(diag, halo, count, x)
        scale[x] = inverse
        scaled_rhs[x] = inverse * rhs[x]
        upper[x] = jnp.where(lane == deep - 1, 0.0, coeff[2, x])
    for x in range(nx):
        for y in range(ny):
            value = full_value(cols, inner, coeff, halo, x, y)
            result = value * row(scale, x, y)
            scaled[x, y] = result
            put(value_stack, x * ny + y, value, row(rhs, x, y))
            put(scaled_stack, x * ny + y, result, row(scaled_rhs, x, y))
    for x in range(nx):
        for y in range(ny):
            over, ahead = row(upper, x, y), pltpu.roll(scaled[x, y], deep - 1, 1)
            pair = over * ahead
            pair_rhs = over * pltpu.roll(jnp.broadcast_to(row(scaled_rhs, x, y), (8, deep)), deep - 1, 1)[:1]
            if x + 1 < nx:
                pair += row(coeff, 0, x, y) * scaled[x + 1, y]
                pair_rhs += row(coeff, 0, x, y) * row(scaled_rhs, x + 1, y)
            if y + 1 < ny:
                pair += row(coeff, 1, x, y) * scaled[x, y + 1]
                pair_rhs += row(coeff, 1, x, y) * row(scaled_rhs, x, y + 1)
            put(pair_stack, x * ny + y, pair, pair_rhs)
    gram, projected = fold(by_rows(basis_stack[...], value_stack[...]), count)
    square, square_rhs = fold(by_rows(value_stack[...], scaled_stack[...]), count)
    pairs, pairs_rhs = fold(by_rows(scaled_stack[...], pair_stack[...]), count)
    part[...] = jnp.zeros_like(part)
    part[pl.ds(0, count), pl.ds(0, count)] = gram
    part[:, pl.ds(count, count)] = square
    part[:, pl.ds(2 * count, count)] = pairs
    part[pl.ds(0, count), pl.ds(3 * count, 1)] = projected
    part[:, pl.ds(3 * count + 1, 1)] = square_rhs
    part[:, pl.ds(3 * count + 2, 1)] = pairs_rhs


def local_sums(cols, inner, basis_stack, coeff, diag, rhs, halo):
    nx, ny, count, deep = cols.shape
    cells = nx * ny * deep
    tall = 2 * count + EXTRA
    small = pltpu.VMEM((nx, ny, deep), F32)
    outs = (shape(count + 8, -(-(3 * count + 3) // LANES) * LANES), shape(tall, cells, dtype=BF16))
    return call(
        local_kernel,
        outs,
        [VM] * 10,
        [
            pltpu.VMEM((tall, cells), BF16),
            pltpu.VMEM((tall, cells), BF16),
            pltpu.VMEM((nx, ny, count, deep), F32),
            small, small, small,
        ],
        limit=28,
        work=60 * count * cells,
        moved=24 * count * cells,
    )(cols, inner, basis_stack, coeff, diag, rhs, *halo)


def shared_kernel(part, scaled_stack, coeff, ya, yb, far_x, far_y, total, mine, pair_stack):
    odd = parity()
    halo = Halo(odd, (None, None, ya, yb))
    count = part.shape[0] - 8
    nx, ny, deep = coeff.shape[1:]
    for y in range(ny):
        face = row(coeff, 0, nx - 1, y)
        put(
            pair_stack, y, face * far_x[pl.ds(y * count, count), :],
            face * far_x[pl.ds(ny * count + y, 1), :],
        )
        mine[:, pl.ds(y * deep, deep)] = scaled_stack[:, pl.ds(((nx - 1) * ny + y) * deep, deep)]
    for x in range(nx):
        own = halo.rows(1, False, nx * count + x, 1)
        face = jnp.where(odd[0] == 0, row(coeff, 1, x, ny - 1), own)
        put(
            pair_stack, ny + x, face * far_y[pl.ds(x * count, count), :],
            face * far_y[pl.ds(nx * count + x, 1), :],
        )

    def side(y):
        for x in range(nx):
            mine[:, pl.ds((ny + x) * deep, deep)] = scaled_stack[:, pl.ds((x * ny + y) * deep, deep)]

    @pl.when(odd[0] == 0)
    def _():
        side(ny - 1)

    @pl.when(odd[0] == 1)
    def _():
        side(0)

    pairs, pairs_rhs = fold(by_rows(mine[...], pair_stack[...]), count)
    total[...] = part[...]
    total[:, pl.ds(2 * count, count)] += pairs
    total[:, pl.ds(3 * count + 2, 1)] += pairs_rhs


def shared_sums(part, scaled_stack, coeff, ya, yb, far_x, far_y):
    nx, ny, deep = coeff.shape[1:]
    wide = pltpu.VMEM((scaled_stack.shape[0], (nx + ny) * deep), BF16)
    return call(
        shared_kernel, shape(*part.shape), [VM] * 7, [wide, wide], limit=12
    )(part, scaled_stack, coeff, ya, yb, far_x, far_y)


def inverse_two(a, b, c, d):
    scale = 1.0 / (a * d - b * c)
    return d * scale, -b * scale, -c * scale, a * scale


def apply_two(matrix, first, second):
    a, b, c, d = matrix
    return a * first + b * second, c * first + d * second


def finish_kernel(total, basis_stack, scaled_stack, guess, stepped):
    count = total.shape[0] - 8
    nx, ny, deep = guess.shape
    sums = total[pl.ds(0, count), :]
    level = lax.broadcasted_iota(jnp.int32, (count, 1), 0)
    lane = lax.broadcasted_iota(jnp.int32, sums.shape, 1)
    own = jnp.where(lane == level, sums, 0.0)
    of_row = lax.rsqrt(jnp.sum(own, axis=1, keepdims=True))
    of_lane = lax.rsqrt(jnp.sum(own, axis=0, keepdims=True))
    work = sums * of_row * jnp.where(lane[:1] < count, of_lane, 1.0)
    for k in range(0, count, 4):
        columns = [jnp.broadcast_to(work[:, k + b : k + b + 1], work.shape) for b in range(4)]
        rows = [work[k + a : k + a + 1, :] for a in range(4)]
        pivot = [[column[k + a : k + a + 1, :] for column in columns] for a in range(4)]
        top = inverse_two(pivot[0][0], pivot[0][1], pivot[1][0], pivot[1][1])
        line_0, line_1 = apply_two(top, rows[0], rows[1])
        across = [apply_two(top, pivot[0][b], pivot[1][b]) for b in (2, 3)]
        low = [rows[a] - pivot[a][0] * line_0 - pivot[a][1] * line_1 for a in (2, 3)]
        rest = [
            [pivot[a][b] - pivot[a][0] * across[b - 2][0] - pivot[a][1] * across[b - 2][1] for b in (2, 3)]
            for a in (2, 3)
        ]
        line_2, line_3 = apply_two(inverse_two(*rest[0], *rest[1]), *low)
        line_0 = line_0 - across[0][0] * line_2 - across[1][0] * line_3
        line_1 = line_1 - across[0][1] * line_2 - across[1][1] * line_3
        lines = (line_0, line_1, line_2, line_3)
        for a in range(4):
            work = work - columns[a] * lines[a]
        for a in range(4):
            work = jnp.where(level == k + a, lines[a], work)
    at = 3 * count
    work = work * of_row
    turned = work.T
    weights = work[:, at : at + 1]
    weights_row = turned[at : at + 1, :]
    shift_row = turned[at + 1 : at + 2, :] - jnp.sum(weights * turned[count : 2 * count, :], axis=0, keepdims=True)
    sums_row = sums.T
    rhs_row = sums_row[at + 1 : at + 2, :]
    both = jnp.sum(weights * sums, axis=0, keepdims=True)
    correction = rhs_row - both[:, count : 2 * count]
    along = jnp.sum(weights_row * (rhs_row + correction), axis=1, keepdims=True)
    tail = total[pl.ds(count, 1), :]
    size = tail[:, at + 1 : at + 2] - along
    crossing = jnp.sum(
        weights_row * (both[:, 2 * count : at] - sums_row[at + 2 : at + 3, :] - tail[:, 2 * count : at]),
        axis=1, keepdims=True,
    ) + tail[:, at + 2 : at + 3]
    lost = jnp.sum(correction * shift_row, axis=1, keepdims=True)
    step = size / (size - 2.0 * crossing - lost)
    first = lax.broadcasted_iota(jnp.int32, (EXTRA, count), 0)
    of_basis = jnp.where(first == 0, weights_row, jnp.where(first == 1, weights_row - step * shift_row, 0.0))
    of_scaled = jnp.where(first == 1, -step * weights_row, 0.0)
    last = lax.broadcasted_iota(jnp.int32, (EXTRA, EXTRA), 0)
    place = lax.broadcasted_iota(jnp.int32, (EXTRA, EXTRA), 1)
    of_rhs = jnp.where((last == 1) & (place < 2), step, 0.0)
    basis_high, basis_low = halves(jnp.concatenate([of_basis, of_basis], axis=1))
    scaled_high, scaled_low = halves(jnp.concatenate([of_scaled, of_scaled, of_rhs], axis=1))
    for x in range(nx):
        lanes = pl.ds(x * ny * deep, ny * deep)
        fields = basis_stack[:, lanes]
        result = jnp.dot(basis_high, fields, preferred_element_type=F32)
        result += jnp.dot(basis_low, fields, preferred_element_type=F32)
        fields = scaled_stack[:, lanes]
        result += jnp.dot(scaled_high, fields, preferred_element_type=F32)
        result += jnp.dot(scaled_low, fields, preferred_element_type=F32)
        for y in range(ny):
            guess[x, pl.ds(y, 1), :] = result[0:1, y * deep : (y + 1) * deep]
            stepped[x, pl.ds(y, 1), :] = result[1:2, y * deep : (y + 1) * deep]


def finish(total, basis_stack, scaled_stack, block):
    return call(finish_kernel, (shape(*block),) * 2, [VM] * 3, limit=24)(
        total, basis_stack, scaled_stack
    )


def steps(basis, rhs, extra_diag, coeff):
    first_x, second_x, first_y, second_y, cols = faces(basis, coeff)
    first_x = swap(first_x, "gx", 0)
    second_x = swap(second_x, "gx", 1)
    first_y = swap(first_y, "gy", 0)
    second_y = swap(second_y, "gy", 1)
    inner, basis_stack, diag = inside(cols, coeff, extra_diag)
    halo = (first_x, second_x, first_y, second_y)
    face_x, face_y = border(cols, inner, coeff, diag, rhs, halo)
    wide, deep = lax.axis_size("gx"), lax.axis_size("gy")
    route = []
    for i in range(wide):
        step = 1 if i % 2 else -1
        route += [(i * deep + j, i * deep + j + step) for j in range(deep) if 0 <= j + step < deep]
    far_y = lax.ppermute(face_y, ("gx", "gy"), route)
    far_x = send(face_x, "gx", -1)
    part, scaled_stack = local_sums(cols, inner, basis_stack, coeff, diag, rhs, halo)
    part = shared_sums(part, scaled_stack, coeff, first_y, second_y, far_x, far_y)
    total = sum_all(part)
    return finish(total, basis_stack, scaled_stack, rhs.shape)


def solution(mesh):
    placed = (
        P(None, "gx", "gy", None),
        P("gx", "gy", None),
        P("gx", "gy", None),
        P(None, "gx", "gy", None),
    )
    return jax.shard_map(
        steps,
        mesh=mesh,
        in_specs=placed,
        out_specs=(P("gx", "gy", None), P("gx", "gy", None)),
        check_vma=False,
    )
```

```python
import functools
import jax
import jax.numpy as jnp
from jax import lax
from jax.experimental import pallas as pl
from jax.experimental.pallas import tpu as pltpu
from jax.sharding import PartitionSpec as P

F32 = jnp.float32
BF16 = jnp.bfloat16
EXTRA = 16
LANES = 128
VM = pl.BlockSpec(memory_space=pltpu.VMEM)
RAW = pl.BlockSpec(memory_space=pl.ANY)


def shape(*dims, dtype=F32):
    return jax.ShapeDtypeStruct(dims, dtype)


def call(body, outs, ins, scratch=(), limit=24, work=0, moved=0):
    return pl.pallas_call(
        body,
        out_shape=outs,
        in_specs=ins,
        out_specs=jax.tree.map(lambda _: VM, outs),
        scratch_shapes=list(scratch),
        compiler_params=pltpu.CompilerParams(vmem_limit_bytes=limit << 20),
        cost_estimate=pl.CostEstimate(flops=work, bytes_accessed=moved, transcendentals=0),
    )


def sum_stages():
    wide, deep = lax.axis_size("gx"), lax.axis_size("gy")
    along_x = [(1 << k, 0) for k in range(wide.bit_length() - 1)]
    along_y = [(0, 1 << k) for k in range(deep.bit_length() - 1)]
    steps = along_y[:0:-1] + along_x + along_y[:1]
    single = len(steps) % 2
    stages = [[step] for step in steps[:single]]
    for at in range(single, len(steps), 2):
        (a, b), (c, d) = steps[at], steps[at + 1]
        stages.append([(a, b), (c, d), (a ^ c, b ^ d)])
    return stages


def sum_all(part):
    wide, deep = lax.axis_size("gx"), lax.axis_size("gy")
    if wide & (wide - 1) or deep & (deep - 1):
        return lax.psum(part, ("gx", "gy"))
    devices = [(i, j) for i in range(wide) for j in range(deep)]
    for stage in sum_stages():
        others = [
            lax.ppermute(
                part,
                ("gx", "gy"),
                [(i * deep + j, (i ^ a) * deep + (j ^ b)) for i, j in devices],
            )
            for a, b in stage
        ]
        for other in others:
            part = part + other
    return part


def send(block, axis, step):
    size = lax.axis_size(axis)
    return lax.ppermute(block, axis, [(i, i + step) for i in range(size) if 0 <= i + step < size])


def swap(block, axis, start):
    size = lax.axis_size(axis)
    pairs = [(i, i + 1) for i in range(start, size - 1, 2)]
    return lax.ppermute(block, axis, pairs + [(j, i) for i, j in pairs])


def halves(value):
    high = value.astype(BF16)
    return high, (value - high.astype(F32)).astype(BF16)


def put(stack, at, value, extra=None):
    count, deep = value.shape
    lanes = pl.ds(at * deep if isinstance(at, int) else pl.multiple_of(at * deep, deep), deep)
    high, low = halves(value)
    stack[pl.ds(0, count), lanes] = high
    stack[pl.ds(count, count), lanes] = low
    if extra is not None:
        stack[pl.ds(2 * count, EXTRA), lanes] = extra


def by_rows(left, right):
    return lax.dot_general(left, right, (((1,), (1,)), ((), ())), preferred_element_type=F32)


OF_RHS, OF_SCALED, OF_PAIR = 0, 2, 4


def fold(full, count, left, right):
    rows = full[:count] + full[count : 2 * count]
    if left is not None:
        at = 2 * count + left
        last = full[at : at + 1] + full[at + 1 : at + 2]
        rows = jnp.concatenate([rows, jnp.broadcast_to(last, (8, full.shape[1]))], axis=0)
    at = 2 * count + right
    return rows[:, :count] + rows[:, count : 2 * count], rows[:, at : at + 1] + rows[:, at + 1 : at + 2]


def parity():
    return lax.axis_index("gx") % 2, lax.axis_index("gy") % 2


def faces_kernel(basis, coeff, first_x, second_x, first_y, second_y, cols, slabs, sems):
    count, nx, ny, _ = basis.shape
    odd = parity()
    copies = [pltpu.make_async_copy(basis.at[:, x], slabs.at[x], sems.at[x]) for x in range(nx)]
    ends = []
    for target in (first_x, second_x):
        ends.append((coeff.at[0, nx - 1], target.at[pl.ds(ny * count, ny)]))
    for target in (first_y, second_y):
        ends.append((coeff.at[1, :, ny - 1, :], target.at[pl.ds(nx * count, nx)]))
    ends = [pltpu.make_async_copy(a, b, sems.at[nx + k]) for k, (a, b) in enumerate(ends)]
    for copy in copies + ends:
        copy.start()
    for x in range(nx):
        copies[x].wait()
        slab = jnp.swapaxes(slabs[x], 0, 1)
        cols[x] = slab
        rows = pl.ds(x * count, count)
        first_y[rows, :] = jnp.where(odd[1] == 0, slab[ny - 1], slab[0])
        second_y[rows, :] = jnp.where(odd[1] == 0, slab[0], slab[ny - 1])
    for y in range(ny):
        rows = pl.ds(y * count, count)
        first_x[rows, :] = jnp.where(odd[0] == 0, cols[nx - 1, y], cols[0, y])
        second_x[rows, :] = jnp.where(odd[0] == 0, cols[0, y], cols[nx - 1, y])
    for copy in ends:
        copy.wait()


def faces(basis, coeff):
    count, nx, ny, deep = basis.shape
    of_x, of_y = shape(ny * count + ny, deep), shape(nx * count + nx, deep)
    outs = (of_x, of_x, of_y, of_y, shape(nx, ny, count, deep))
    slabs = pltpu.VMEM((nx, count, ny, deep), F32)
    sems = pltpu.SemaphoreType.DMA((nx + 4,))
    return call(faces_kernel, outs, [RAW, RAW], [slabs, sems], limit=50)(basis, coeff)


def row(ref, *at):
    return ref[at[:-1] + (pl.ds(at[-1], 1), slice(None))]


def near_z(field, upper, lower):
    deep = field.shape[1]
    above, below = pltpu.roll(field, deep - 1, 1), pltpu.roll(field, 1, 1)
    return upper * above + lower * below


def inner_kernel(cols, coeff, extra_raw, inner, stack, diag, upper, lower, ahead, behind, extra, sem):
    nx, ny, _, deep = cols.shape
    extra_copy = pltpu.make_async_copy(extra_raw, extra, sem)
    extra_copy.start()
    level = lax.broadcasted_iota(jnp.int32, (ny, deep), 0)
    lane = lax.broadcasted_iota(jnp.int32, (ny, deep), 1)
    extra_copy.wait()
    for x in range(nx):
        cx, cy, cz = coeff[0, x], coeff[1, x], coeff[2, x]
        upper[x] = jnp.where(lane == deep - 1, 0.0, cz)
        under = jnp.where(lane == 0, 0.0, pltpu.roll(cz, 1, 1))
        lower[x] = under
        before = coeff[0, x - 1] if x else jnp.zeros_like(cx)
        behind[x] = before
        ahead[x] = cx if x + 1 < nx else jnp.zeros_like(cx)
        total = extra[x] + cx + cy + cz + under + before
        diag[x] = total + jnp.where(level == 0, 0.0, pltpu.roll(cy, 1, 0))

    def slab(x, carry):
        after, before = jnp.minimum(x + 1, nx - 1), jnp.maximum(x - 1, 0)
        for y in range(ny):
            here = cols[x, y]
            sums = near_z(here, row(upper, x, y), row(lower, x, y))
            sums += row(ahead, x, y) * cols[after, y]
            sums += row(behind, x, y) * cols[before, y]
            if y + 1 < ny:
                sums += row(coeff, 1, x, y) * cols[x, y + 1]
            if y:
                sums += row(coeff, 1, x, y - 1) * cols[x, y - 1]
            inner[x, y] = row(diag, x, y) * here - sums
            put(stack, x * ny + y, here)
        return carry

    lax.fori_loop(0, nx, slab, 0)


def inside(cols, coeff, extra):
    nx, ny, count, deep = cols.shape
    cells = nx * ny * deep
    outs = (shape(nx, ny, count, deep), shape(2 * count, cells, dtype=BF16), shape(nx, ny, deep))
    small = pltpu.VMEM((nx, ny, deep), F32)
    return call(
        inner_kernel, outs, [VM, VM, RAW], [small] * 5 + [pltpu.SemaphoreType.DMA],
        work=20 * count * cells, moved=16 * count * cells,
    )(cols, coeff, extra)


class Halo:
    def __init__(self, odd, refs):
        self.odd = odd
        self.refs = refs

    def rows(self, axis, upper, start, size):
        first, second = self.refs[2 * axis : 2 * axis + 2]
        here = pl.ds(start, size)
        return jnp.where(self.odd[axis] == (0 if upper else 1), first[here, :], second[here, :])


def inverse_diagonal(diag, halo, count, x):
    nx, ny, deep = diag.shape
    level = lax.broadcasted_iota(jnp.int32, (ny, deep), 0)
    total = diag[x] + jnp.where(level == 0, halo.rows(1, False, nx * count + x, 1), 0.0)
    if x == 0:
        total += halo.rows(0, False, ny * count, ny)
    return 1.0 / total


def full_value(cols, inner, coeff, halo, x, y):
    nx, ny, count, _ = cols.shape
    value = inner[x, y]
    if x == 0:
        value += halo.rows(0, False, ny * count + y, 1) * (cols[x, y] - halo.rows(0, False, y * count, count))
    if x == nx - 1:
        value -= row(coeff, 0, x, y) * halo.rows(0, True, y * count, count)
    if y == 0:
        value += halo.rows(1, False, nx * count + x, 1) * (cols[x, y] - halo.rows(1, False, x * count, count))
    if y == ny - 1:
        value -= row(coeff, 1, x, y) * halo.rows(1, True, x * count, count)
    return value


def border_kernel(cols, inner, coeff, diag, rhs, xa, xb, ya, yb, face_x, face_y, scale):
    nx, ny, count, _ = cols.shape
    odd = parity()
    halo = Halo(odd, (xa, xb, ya, yb))
    for x in range(nx):
        scale[x] = inverse_diagonal(diag, halo, count, x)
    value = functools.partial(full_value, cols, inner, coeff, halo)
    for y in range(ny):
        face_x[pl.ds(y * count, count), :] = value(0, y) * row(scale, 0, y)
    face_x[pl.ds(ny * count, ny), :] = scale[0] * rhs[0]

    def side(y):
        for x in range(nx):
            face_y[pl.ds(x * count, count), :] = value(x, y) * row(scale, x, y)
            face_y[pl.ds(nx * count + x, 1), :] = row(scale, x, y) * row(rhs, x, y)

    @pl.when(odd[0] == 0)
    def _():
        side(0)

    @pl.when(odd[0] == 1)
    def _():
        side(ny - 1)


def border(cols, inner, coeff, diag, rhs, halo):
    nx, ny, count, deep = cols.shape
    outs = (shape(ny * count + ny, deep), shape(nx * count + nx, deep))
    return call(
        border_kernel, outs, [VM] * 9, [pltpu.VMEM((nx, ny, deep), F32)], limit=10
    )(cols, inner, coeff, diag, rhs, *halo)


def local_kernel(
    cols, inner, basis_stack, coeff, diag, rhs, xa, xb, ya, yb,
    part, scaled_stack, value_stack, pair_stack, scaled, scale, upper, scaled_rhs, ends,
):
    nx, ny, count, deep = cols.shape
    odd = parity()
    halo = Halo(odd, (xa, xb, ya, yb))
    lane = lax.broadcasted_iota(jnp.int32, (ny, deep), 1)
    for x in range(nx):
        inverse = inverse_diagonal(diag, halo, count, x)
        scale[x] = inverse
        scaled_rhs[x] = inverse * rhs[x]
        upper[x] = jnp.where(lane == deep - 1, 0.0, coeff[2, x])
    level = lax.broadcasted_iota(jnp.int32, (ny, deep), 0)
    for x in range(nx):
        field = scaled_rhs[x]
        pair = upper[x] * pltpu.roll(field, deep - 1, 1)
        pair += jnp.where(level == ny - 1, 0.0, coeff[1, x] * pltpu.roll(field, ny - 1, 0))
        if x + 1 < nx:
            pair += coeff[0, x] * scaled_rhs[x + 1]
        parts = []
        for full in (rhs[x], field, pair):
            high = full.astype(BF16).astype(F32)
            parts += [high, full - high]
        parts += [jnp.zeros_like(pair)] * 2
        ends[x] = jnp.swapaxes(jnp.stack(parts), 0, 1)
    blank = jnp.zeros((EXTRA - 8, deep), F32)
    for x in range(nx):
        for y in range(ny):
            extra = jnp.concatenate([ends[x, y], blank], axis=0).astype(BF16)
            value = full_value(cols, inner, coeff, halo, x, y)
            result = value * row(scale, x, y)
            scaled[x, y] = result
            put(value_stack, x * ny + y, value, extra)
            put(scaled_stack, x * ny + y, result, extra)
    for x in range(nx):
        for y in range(ny):
            pair = row(upper, x, y) * pltpu.roll(scaled[x, y], deep - 1, 1)
            if x + 1 < nx:
                pair += row(coeff, 0, x, y) * scaled[x + 1, y]
            if y + 1 < ny:
                pair += row(coeff, 1, x, y) * scaled[x, y + 1]
            extra = jnp.concatenate([ends[x, y], blank], axis=0).astype(BF16)
            put(pair_stack, x * ny + y, pair, extra)
    gram, projected = fold(by_rows(basis_stack[...], value_stack[...]), count, None, OF_RHS)
    square, square_rhs = fold(by_rows(value_stack[...], scaled_stack[...]), count, OF_RHS, OF_SCALED)
    pairs, pairs_rhs = fold(by_rows(scaled_stack[...], pair_stack[...]), count, OF_SCALED, OF_PAIR)
    part[...] = jnp.zeros_like(part)
    part[pl.ds(0, count), pl.ds(0, count)] = gram
    part[:, pl.ds(count, count)] = square
    part[:, pl.ds(2 * count, count)] = pairs
    part[pl.ds(0, count), pl.ds(3 * count, 1)] = projected
    part[:, pl.ds(3 * count + 1, 1)] = square_rhs
    part[:, pl.ds(3 * count + 2, 1)] = pairs_rhs


def local_sums(cols, inner, basis_stack, coeff, diag, rhs, halo):
    nx, ny, count, deep = cols.shape
    cells = nx * ny * deep
    tall = 2 * count + EXTRA
    small = pltpu.VMEM((nx, ny, deep), F32)
    outs = (shape(count + 8, -(-(3 * count + 3) // LANES) * LANES), shape(tall, cells, dtype=BF16))
    return call(
        local_kernel,
        outs,
        [VM] * 10,
        [
            pltpu.VMEM((tall, cells), BF16),
            pltpu.VMEM((tall, cells), BF16),
            pltpu.VMEM((nx, ny, count, deep), F32),
            small, small, small,
            pltpu.VMEM((nx, ny, 8, deep), F32),
        ],
        limit=28,
        work=60 * count * cells,
        moved=24 * count * cells,
    )(cols, inner, basis_stack, coeff, diag, rhs, *halo)


def pair_rows(field):
    high = field.astype(BF16).astype(F32)
    at = lax.broadcasted_iota(jnp.int32, (EXTRA, field.shape[1]), 0)
    both = jnp.where(at == OF_PAIR, high, jnp.where(at == OF_PAIR + 1, field - high, 0.0))
    return both.astype(BF16)


def shared_kernel(part, scaled_stack, coeff, ya, yb, far_x, far_y, total, mine, pair_stack):
    odd = parity()
    halo = Halo(odd, (None, None, ya, yb))
    count = part.shape[0] - 8
    nx, ny, deep = coeff.shape[1:]
    for y in range(ny):
        face = row(coeff, 0, nx - 1, y)
        put(
            pair_stack, y, face * far_x[pl.ds(y * count, count), :],
            pair_rows(face * far_x[pl.ds(ny * count + y, 1), :]),
        )
        mine[:, pl.ds(y * deep, deep)] = scaled_stack[:, pl.ds(((nx - 1) * ny + y) * deep, deep)]
    for x in range(nx):
        own = halo.rows(1, False, nx * count + x, 1)
        face = jnp.where(odd[0] == 0, row(coeff, 1, x, ny - 1), own)
        put(
            pair_stack, ny + x, face * far_y[pl.ds(x * count, count), :],
            pair_rows(face * far_y[pl.ds(nx * count + x, 1), :]),
        )

    def side(y):
        for x in range(nx):
            mine[:, pl.ds((ny + x) * deep, deep)] = scaled_stack[:, pl.ds((x * ny + y) * deep, deep)]

    @pl.when(odd[0] == 0)
    def _():
        side(ny - 1)

    @pl.when(odd[0] == 1)
    def _():
        side(0)

    pairs, pairs_rhs = fold(by_rows(mine[...], pair_stack[...]), count, OF_SCALED, OF_PAIR)
    total[...] = part[...]
    total[:, pl.ds(2 * count, count)] += pairs
    total[:, pl.ds(3 * count + 2, 1)] += pairs_rhs


def shared_sums(part, scaled_stack, coeff, ya, yb, far_x, far_y):
    nx, ny, deep = coeff.shape[1:]
    wide = pltpu.VMEM((scaled_stack.shape[0], (nx + ny) * deep), BF16)
    return call(
        shared_kernel, shape(*part.shape), [VM] * 7, [wide, wide], limit=12
    )(part, scaled_stack, coeff, ya, yb, far_x, far_y)


def inverse_two(a, b, c, d):
    scale = 1.0 / (a * d - b * c)
    return d * scale, -b * scale, -c * scale, a * scale


def apply_two(matrix, first, second):
    a, b, c, d = matrix
    return a * first + b * second, c * first + d * second


def output_rows(first, second, width):
    at = lax.broadcasted_iota(jnp.int32, (EXTRA, width), 0)
    both = jnp.where(at % 2 == 0, first, second)
    high = both.astype(BF16).astype(F32)
    return jnp.where(at < 2, high, jnp.where(at < 4, both - high, 0.0))


def finish_kernel(total, basis_stack, scaled_stack, guess, stepped):
    count = total.shape[0] - 8
    nx, ny, deep = guess.shape
    sums = total[pl.ds(0, count), :]
    level = lax.broadcasted_iota(jnp.int32, (count, 1), 0)
    lane = lax.broadcasted_iota(jnp.int32, sums.shape, 1)
    own = jnp.where(lane == level, sums, 0.0)
    of_row = lax.rsqrt(jnp.sum(own, axis=1, keepdims=True))
    of_lane = lax.rsqrt(jnp.sum(own, axis=0, keepdims=True))
    work = sums * of_row * jnp.where(lane[:1] < count, of_lane, 1.0)
    for k in range(0, count, 4):
        columns = [jnp.broadcast_to(work[:, k + b : k + b + 1], work.shape) for b in range(4)]
        rows = [work[k + a : k + a + 1, :] for a in range(4)]
        pivot = [[column[k + a : k + a + 1, :] for column in columns] for a in range(4)]
        top = inverse_two(pivot[0][0], pivot[0][1], pivot[1][0], pivot[1][1])
        line_0, line_1 = apply_two(top, rows[0], rows[1])
        across = [apply_two(top, pivot[0][b], pivot[1][b]) for b in (2, 3)]
        low = [rows[a] - pivot[a][0] * line_0 - pivot[a][1] * line_1 for a in (2, 3)]
        rest = [
            [pivot[a][b] - pivot[a][0] * across[b - 2][0] - pivot[a][1] * across[b - 2][1] for b in (2, 3)]
            for a in (2, 3)
        ]
        line_2, line_3 = apply_two(inverse_two(*rest[0], *rest[1]), *low)
        line_0 = line_0 - across[0][0] * line_2 - across[1][0] * line_3
        line_1 = line_1 - across[0][1] * line_2 - across[1][1] * line_3
        lines = (line_0, line_1, line_2, line_3)
        for a in range(4):
            work = work - columns[a] * lines[a]
        for a in range(4):
            work = jnp.where(level == k + a, lines[a], work)
    at = 3 * count
    work = work * of_row
    turned = work.T
    weights = work[:, at : at + 1]
    weights_row = turned[at : at + 1, :]
    shift_row = turned[at + 1 : at + 2, :] - jnp.sum(weights * turned[count : 2 * count, :], axis=0, keepdims=True)
    sums_row = sums.T
    rhs_row = sums_row[at + 1 : at + 2, :]
    both = jnp.sum(weights * sums, axis=0, keepdims=True)
    correction = rhs_row - both[:, count : 2 * count]
    along = jnp.sum(weights_row * (rhs_row + correction), axis=1, keepdims=True)
    tail = total[pl.ds(count, 1), :]
    size = tail[:, at + 1 : at + 2] - along
    crossing = jnp.sum(
        weights_row * (both[:, 2 * count : at] - sums_row[at + 2 : at + 3, :] - tail[:, 2 * count : at]),
        axis=1, keepdims=True,
    ) + tail[:, at + 2 : at + 3]
    lost = jnp.sum(correction * shift_row, axis=1, keepdims=True)
    step = size / (size - 2.0 * crossing - lost)
    of_basis = output_rows(weights_row, weights_row - step * shift_row, count)
    of_scaled = output_rows(jnp.zeros_like(weights_row), -step * weights_row, count)
    place = lax.broadcasted_iota(jnp.int32, (1, EXTRA), 1)
    of_rhs = jnp.where((place == OF_SCALED) | (place == OF_SCALED + 1), step, 0.0)
    of_rhs = output_rows(jnp.zeros_like(of_rhs), of_rhs, EXTRA)
    of_basis = jnp.concatenate([of_basis, of_basis], axis=1).astype(BF16)
    of_scaled = jnp.concatenate([of_scaled, of_scaled, of_rhs], axis=1).astype(BF16)
    for x in range(nx):
        lanes = pl.ds(x * ny * deep, ny * deep)
        result = jnp.dot(of_basis, basis_stack[:, lanes], preferred_element_type=F32)
        result += jnp.dot(of_scaled, scaled_stack[:, lanes], preferred_element_type=F32)
        result = result[0:2] + result[2:4]
        for y in range(ny):
            guess[x, pl.ds(y, 1), :] = result[0:1, y * deep : (y + 1) * deep]
            stepped[x, pl.ds(y, 1), :] = result[1:2, y * deep : (y + 1) * deep]


def finish(total, basis_stack, scaled_stack, block):
    return call(finish_kernel, (shape(*block),) * 2, [VM] * 3, limit=24)(
        total, basis_stack, scaled_stack
    )


def steps(basis, rhs, extra_diag, coeff):
    first_x, second_x, first_y, second_y, cols = faces(basis, coeff)
    first_x = swap(first_x, "gx", 0)
    second_x = swap(second_x, "gx", 1)
    first_y = swap(first_y, "gy", 0)
    second_y = swap(second_y, "gy", 1)
    inner, basis_stack, diag = inside(cols, coeff, extra_diag)
    halo = (first_x, second_x, first_y, second_y)
    face_x, face_y = border(cols, inner, coeff, diag, rhs, halo)
    wide, deep = lax.axis_size("gx"), lax.axis_size("gy")
    route = []
    for i in range(wide):
        step = 1 if i % 2 else -1
        route += [(i * deep + j, i * deep + j + step) for j in range(deep) if 0 <= j + step < deep]
    far_y = lax.ppermute(face_y, ("gx", "gy"), route)
    far_x = send(face_x, "gx", -1)
    part, scaled_stack = local_sums(cols, inner, basis_stack, coeff, diag, rhs, halo)
    part = shared_sums(part, scaled_stack, coeff, first_y, second_y, far_x, far_y)
    total = sum_all(part)
    return finish(total, basis_stack, scaled_stack, rhs.shape)


def solution(mesh):
    placed = (
        P(None, "gx", "gy", None),
        P("gx", "gy", None),
        P("gx", "gy", None),
        P(None, "gx", "gy", None),
    )
    return jax.shard_map(
        steps,
        mesh=mesh,
        in_specs=placed,
        out_specs=(P("gx", "gy", None), P("gx", "gy", None)),
        check_vma=False,
    )
```

```python
import functools
import jax
import jax.numpy as jnp
from jax import lax
from jax.experimental import pallas as pl
from jax.experimental.pallas import tpu as pltpu
from jax.sharding import PartitionSpec as P

F32 = jnp.float32
BF16 = jnp.bfloat16
EXTRA = 16
LANES = 128
VM = pl.BlockSpec(memory_space=pltpu.VMEM)
RAW = pl.BlockSpec(memory_space=pl.ANY)


def shape(*dims, dtype=F32):
    return jax.ShapeDtypeStruct(dims, dtype)


def call(body, outs, ins, scratch=(), limit=24, work=0, moved=0):
    return pl.pallas_call(
        body,
        out_shape=outs,
        in_specs=ins,
        out_specs=jax.tree.map(lambda _: VM, outs),
        scratch_shapes=list(scratch),
        compiler_params=pltpu.CompilerParams(vmem_limit_bytes=limit << 20),
        cost_estimate=pl.CostEstimate(flops=work, bytes_accessed=moved, transcendentals=0),
    )


def sum_stages():
    wide, deep = lax.axis_size("gx"), lax.axis_size("gy")
    along_x = [(1 << k, 0) for k in range(wide.bit_length() - 1)]
    along_y = [(0, 1 << k) for k in range(deep.bit_length() - 1)]
    steps = along_y[:0:-1] + along_x + along_y[:1]
    single = len(steps) % 2
    stages = [[step] for step in steps[:single]]
    for at in range(single, len(steps), 2):
        (a, b), (c, d) = steps[at], steps[at + 1]
        stages.append([(a, b), (c, d), (a ^ c, b ^ d)])
    return stages


def sum_all(part):
    wide, deep = lax.axis_size("gx"), lax.axis_size("gy")
    if wide & (wide - 1) or deep & (deep - 1):
        return lax.psum(part, ("gx", "gy"))
    devices = [(i, j) for i in range(wide) for j in range(deep)]
    for stage in sum_stages():
        others = [
            lax.ppermute(
                part,
                ("gx", "gy"),
                [(i * deep + j, (i ^ a) * deep + (j ^ b)) for i, j in devices],
            )
            for a, b in stage
        ]
        for other in others:
            part = part + other
    return part


def send(block, axis, step):
    size = lax.axis_size(axis)
    return lax.ppermute(block, axis, [(i, i + step) for i in range(size) if 0 <= i + step < size])


def swap(block, axis, start):
    size = lax.axis_size(axis)
    pairs = [(i, i + 1) for i in range(start, size - 1, 2)]
    return lax.ppermute(block, axis, pairs + [(j, i) for i, j in pairs])


def halves(value):
    high = value.astype(BF16)
    return high, (value - high.astype(F32)).astype(BF16)


def put(stack, at, value, extra=None):
    count, deep = value.shape
    lanes = pl.ds(at * deep if isinstance(at, int) else pl.multiple_of(at * deep, deep), deep)
    high, low = halves(value)
    stack[pl.ds(0, count), lanes] = high
    stack[pl.ds(count, count), lanes] = low
    if extra is not None:
        stack[pl.ds(2 * count, EXTRA), lanes] = extra


def by_rows(left, right):
    return lax.dot_general(left, right, (((1,), (1,)), ((), ())), preferred_element_type=F32)


OF_RHS, OF_SCALED, OF_PAIR = 0, 2, 4


def fold(full, count, left, right):
    rows = full[:count] + full[count : 2 * count]
    if left is not None:
        at = 2 * count + left
        last = full[at : at + 1] + full[at + 1 : at + 2]
        rows = jnp.concatenate([rows, jnp.broadcast_to(last, (8, full.shape[1]))], axis=0)
    at = 2 * count + right
    return rows[:, :count] + rows[:, count : 2 * count], rows[:, at : at + 1] + rows[:, at + 1 : at + 2]


def parity():
    return lax.axis_index("gx") % 2, lax.axis_index("gy") % 2


def faces_kernel(basis, coeff, first_x, second_x, first_y, second_y, cols, slabs, sems):
    count, nx, ny, _ = basis.shape
    odd = parity()
    copies = [pltpu.make_async_copy(basis.at[:, x], slabs.at[x], sems.at[x]) for x in range(nx)]
    ends = []
    for target in (first_x, second_x):
        ends.append((coeff.at[0, nx - 1], target.at[pl.ds(ny * count, ny)]))
    for target in (first_y, second_y):
        ends.append((coeff.at[1, :, ny - 1, :], target.at[pl.ds(nx * count, nx)]))
    ends = [pltpu.make_async_copy(a, b, sems.at[nx + k]) for k, (a, b) in enumerate(ends)]
    for copy in copies + ends:
        copy.start()
    for x in range(nx):
        copies[x].wait()
        slab = jnp.swapaxes(slabs[x], 0, 1)
        cols[x] = slab
        rows = pl.ds(x * count, count)
        first_y[rows, :] = jnp.where(odd[1] == 0, slab[ny - 1], slab[0])
        second_y[rows, :] = jnp.where(odd[1] == 0, slab[0], slab[ny - 1])
    for y in range(ny):
        rows = pl.ds(y * count, count)
        first_x[rows, :] = jnp.where(odd[0] == 0, cols[nx - 1, y], cols[0, y])
        second_x[rows, :] = jnp.where(odd[0] == 0, cols[0, y], cols[nx - 1, y])
    for copy in ends:
        copy.wait()


def faces(basis, coeff):
    count, nx, ny, deep = basis.shape
    of_x, of_y = shape(ny * count + ny, deep), shape(nx * count + nx, deep)
    outs = (of_x, of_x, of_y, of_y, shape(nx, ny, count, deep))
    slabs = pltpu.VMEM((nx, count, ny, deep), F32)
    sems = pltpu.SemaphoreType.DMA((nx + 4,))
    return call(faces_kernel, outs, [RAW, RAW], [slabs, sems], limit=50)(basis, coeff)


def row(ref, *at):
    return ref[at[:-1] + (pl.ds(at[-1], 1), slice(None))]


def near_z(field, upper, lower):
    deep = field.shape[1]
    above, below = pltpu.roll(field, deep - 1, 1), pltpu.roll(field, 1, 1)
    return upper * above + lower * below


def outer_columns(nx, ny):
    ends = [(x, y) for x in range(1, nx - 1) for y in (0, ny - 1)]
    return [(x, y) for x in (0, nx - 1) for y in range(ny)] + ends


def end_rows(fields):
    parts = []
    for full in fields:
        high = full.astype(BF16).astype(F32)
        parts += [high, full - high]
    parts += [jnp.zeros_like(parts[0])] * (8 - len(parts))
    return jnp.swapaxes(jnp.stack(parts), 0, 1)


def end_block(rows):
    blank = jnp.zeros((EXTRA - rows.shape[0], rows.shape[1]), F32)
    return jnp.concatenate([rows, blank], axis=0).astype(BF16)


def inner_kernel(
    cols, coeff, rhs, extra_raw,
    inner, inside_basis, outside_basis, inside_scaled, scaled, diag, gram, square,
    upper, lower, ahead, behind, extra, ends, inside_value, sem,
):
    nx, ny, _, deep = cols.shape
    extra_copy = pltpu.make_async_copy(extra_raw, extra, sem)
    extra_copy.start()
    level = lax.broadcasted_iota(jnp.int32, (ny, deep), 0)
    lane = lax.broadcasted_iota(jnp.int32, (ny, deep), 1)
    extra_copy.wait()
    for x in range(nx):
        cx, cy, cz = coeff[0, x], coeff[1, x], coeff[2, x]
        upper[x] = jnp.where(lane == deep - 1, 0.0, cz)
        under = jnp.where(lane == 0, 0.0, pltpu.roll(cz, 1, 1))
        lower[x] = under
        before = coeff[0, x - 1] if x else jnp.zeros_like(cx)
        behind[x] = before
        ahead[x] = cx if x + 1 < nx else jnp.zeros_like(cx)
        total = extra[x] + cx + cy + cz + under + before
        diag[x] = total + jnp.where(level == 0, 0.0, pltpu.roll(cy, 1, 0))

    def slab(x, carry):
        after, before = jnp.minimum(x + 1, nx - 1), jnp.maximum(x - 1, 0)
        for y in range(ny):
            here = cols[x, y]
            sums = near_z(here, row(upper, x, y), row(lower, x, y))
            sums += row(ahead, x, y) * cols[after, y]
            sums += row(behind, x, y) * cols[before, y]
            if y + 1 < ny:
                sums += row(coeff, 1, x, y) * cols[x, y + 1]
            if y:
                sums += row(coeff, 1, x, y - 1) * cols[x, y - 1]
            inner[x, y] = row(diag, x, y) * here - sums
        return carry

    def middle(x, carry):
        scale = 1.0 / diag[x]
        ends[...] = end_rows((rhs[x], scale * rhs[x]))
        behind[x] = scale
        for y in range(1, ny - 1):
            at = (x - 1) * (ny - 2) + y - 1
            block = end_block(ends[y])
            value = inner[x, y]
            result = value * row(behind, x, y)
            scaled[x, y] = result
            put(inside_basis, at, cols[x, y])
            put(inside_value, at, value, block)
            put(inside_scaled, at, result, block)
        return carry

    lax.fori_loop(0, nx, slab, 0)
    lax.fori_loop(1, nx - 1, middle, 0)
    for at, (x, y) in enumerate(outer_columns(nx, ny)):
        put(outside_basis, at, cols[x, y])
    gram[...] = by_rows(inside_basis[...], inside_value[...])
    square[...] = by_rows(inside_value[...], inside_scaled[...])


def inside(cols, coeff, rhs, extra):
    nx, ny, count, deep = cols.shape
    cells = nx * ny * deep
    tall = 2 * count + EXTRA
    outer = len(outer_columns(nx, ny)) * deep
    full = shape(nx, ny, count, deep)
    outs = (
        full,
        shape(2 * count, cells - outer, dtype=BF16),
        shape(2 * count, outer, dtype=BF16),
        shape(tall, cells - outer, dtype=BF16),
        full,
        shape(nx, ny, deep),
        shape(2 * count, tall),
        shape(tall, tall),
    )
    small = pltpu.VMEM((nx, ny, deep), F32)
    scratch = [small] * 5 + [
        pltpu.VMEM((ny, 8, deep), F32),
        pltpu.VMEM((tall, cells - outer), BF16),
        pltpu.SemaphoreType.DMA,
    ]
    return call(
        inner_kernel, outs, [VM, VM, VM, RAW], scratch, work=60 * count * cells, moved=24 * count * cells
    )(cols, coeff, rhs, extra)


class Halo:
    def __init__(self, odd, refs):
        self.odd = odd
        self.refs = refs

    def rows(self, axis, upper, start, size):
        first, second = self.refs[2 * axis : 2 * axis + 2]
        here = pl.ds(start, size)
        return jnp.where(self.odd[axis] == (0 if upper else 1), first[here, :], second[here, :])


def inverse_diagonal(diag, halo, count, x):
    nx, ny, deep = diag.shape
    level = lax.broadcasted_iota(jnp.int32, (ny, deep), 0)
    total = diag[x] + jnp.where(level == 0, halo.rows(1, False, nx * count + x, 1), 0.0)
    if x == 0:
        total += halo.rows(0, False, ny * count, ny)
    return 1.0 / total


def full_value(cols, inner, coeff, halo, x, y):
    nx, ny, count, _ = cols.shape
    value = inner[x, y]
    if x == 0:
        value += halo.rows(0, False, ny * count + y, 1) * (cols[x, y] - halo.rows(0, False, y * count, count))
    if x == nx - 1:
        value -= row(coeff, 0, x, y) * halo.rows(0, True, y * count, count)
    if y == 0:
        value += halo.rows(1, False, nx * count + x, 1) * (cols[x, y] - halo.rows(1, False, x * count, count))
    if y == ny - 1:
        value -= row(coeff, 1, x, y) * halo.rows(1, True, x * count, count)
    return value


def border_kernel(cols, inner, coeff, diag, rhs, xa, xb, ya, yb, face_x, face_y, scale):
    nx, ny, count, _ = cols.shape
    odd = parity()
    halo = Halo(odd, (xa, xb, ya, yb))
    for x in range(nx):
        scale[x] = inverse_diagonal(diag, halo, count, x)
    value = functools.partial(full_value, cols, inner, coeff, halo)
    for y in range(ny):
        face_x[pl.ds(y * count, count), :] = value(0, y) * row(scale, 0, y)
    face_x[pl.ds(ny * count, ny), :] = scale[0] * rhs[0]

    def side(y):
        for x in range(nx):
            face_y[pl.ds(x * count, count), :] = value(x, y) * row(scale, x, y)
            face_y[pl.ds(nx * count + x, 1), :] = row(scale, x, y) * row(rhs, x, y)

    @pl.when(odd[0] == 0)
    def _():
        side(0)

    @pl.when(odd[0] == 1)
    def _():
        side(ny - 1)


def border(cols, inner, coeff, diag, rhs, halo):
    nx, ny, count, deep = cols.shape
    outs = (shape(ny * count + ny, deep), shape(nx * count + nx, deep))
    return call(
        border_kernel, outs, [VM] * 9, [pltpu.VMEM((nx, ny, deep), F32)], limit=10
    )(cols, inner, coeff, diag, rhs, *halo)


def local_kernel(
    cols, inner, outside_basis, inside_scaled, scaled, gram_in, square_in, coeff, diag, rhs, xa, xb, ya, yb,
    part, outside_scaled, outside_value, inside_pair, outside_pair, border, scale, upper, scaled_rhs, ends,
):
    nx, ny, count, deep = cols.shape
    odd = parity()
    halo = Halo(odd, (xa, xb, ya, yb))
    lane = lax.broadcasted_iota(jnp.int32, (ny, deep), 1)
    level = lax.broadcasted_iota(jnp.int32, (ny, deep), 0)
    for x in range(nx):
        inverse = inverse_diagonal(diag, halo, count, x)
        scale[x] = inverse
        scaled_rhs[x] = inverse * rhs[x]
        upper[x] = jnp.where(lane == deep - 1, 0.0, coeff[2, x])
    for x in range(nx):
        field = scaled_rhs[x]
        pair = upper[x] * pltpu.roll(field, deep - 1, 1)
        pair += jnp.where(level == ny - 1, 0.0, coeff[1, x] * pltpu.roll(field, ny - 1, 0))
        if x + 1 < nx:
            pair += coeff[0, x] * scaled_rhs[x + 1]
        ends[x] = end_rows((rhs[x], field, pair))
    outer = {place: at for at, place in enumerate(outer_columns(nx, ny))}
    for (x, y), at in outer.items():
        block = end_block(ends[x, y])
        value = full_value(cols, inner, coeff, halo, x, y)
        result = value * row(scale, x, y)
        border[at] = result
        put(outside_value, at, value, block)
        put(outside_scaled, at, result, block)

    def field_at(x, y):
        return border[outer[x, y]] if (x, y) in outer else scaled[x, y]

    for x in range(nx):
        for y in range(ny):
            pair = row(upper, x, y) * pltpu.roll(field_at(x, y), deep - 1, 1)
            if x + 1 < nx:
                pair += row(coeff, 0, x, y) * field_at(x + 1, y)
            if y + 1 < ny:
                pair += row(coeff, 1, x, y) * field_at(x, y + 1)
            block = end_block(ends[x, y])
            if (x, y) in outer:
                put(outside_pair, outer[x, y], pair, block)
            else:
                put(inside_pair, (x - 1) * (ny - 2) + y - 1, pair, block)
    gram = gram_in[...] + by_rows(outside_basis[...], outside_value[...])
    gram, projected = fold(gram, count, None, OF_RHS)
    square = square_in[...] + by_rows(outside_value[...], outside_scaled[...])
    square, square_rhs = fold(square, count, OF_RHS, OF_SCALED)
    pairs = by_rows(inside_scaled[...], inside_pair[...]) + by_rows(outside_scaled[...], outside_pair[...])
    pairs, pairs_rhs = fold(pairs, count, OF_SCALED, OF_PAIR)
    part[...] = jnp.zeros_like(part)
    part[pl.ds(0, count), pl.ds(0, count)] = gram
    part[:, pl.ds(count, count)] = square
    part[:, pl.ds(2 * count, count)] = pairs
    part[pl.ds(0, count), pl.ds(3 * count, 1)] = projected
    part[:, pl.ds(3 * count + 1, 1)] = square_rhs
    part[:, pl.ds(3 * count + 2, 1)] = pairs_rhs


def local_sums(cols, inner, outside_basis, inside_scaled, scaled, gram, square, coeff, diag, rhs, halo):
    nx, ny, count, deep = cols.shape
    cells = nx * ny * deep
    tall = 2 * count + EXTRA
    columns = len(outer_columns(nx, ny))
    outer = columns * deep
    small = pltpu.VMEM((nx, ny, deep), F32)
    width = -(-(3 * count + 3) // LANES) * LANES
    return call(
        local_kernel,
        (shape(count + 8, width), shape(tall, outer, dtype=BF16)),
        [VM] * 14,
        [
            pltpu.VMEM((tall, outer), BF16),
            pltpu.VMEM((tall, cells - outer), BF16),
            pltpu.VMEM((tall, outer), BF16),
            pltpu.VMEM((columns, count, deep), F32),
            small, small, small,
            pltpu.VMEM((nx, ny, 8, deep), F32),
        ],
        limit=28,
        work=60 * count * cells,
        moved=24 * count * cells,
    )(cols, inner, outside_basis, inside_scaled, scaled, gram, square, coeff, diag, rhs, *halo)


def pair_rows(field):
    high = field.astype(BF16).astype(F32)
    at = lax.broadcasted_iota(jnp.int32, (EXTRA, field.shape[1]), 0)
    both = jnp.where(at == OF_PAIR, high, jnp.where(at == OF_PAIR + 1, field - high, 0.0))
    return both.astype(BF16)


def shared_kernel(part, scaled_stack, coeff, ya, yb, far_x, far_y, total, mine, pair_stack):
    odd = parity()
    halo = Halo(odd, (None, None, ya, yb))
    count = part.shape[0] - 8
    nx, ny, deep = coeff.shape[1:]
    outer = {place: at for at, place in enumerate(outer_columns(nx, ny))}
    for y in range(ny):
        face = row(coeff, 0, nx - 1, y)
        put(
            pair_stack, y, face * far_x[pl.ds(y * count, count), :],
            pair_rows(face * far_x[pl.ds(ny * count + y, 1), :]),
        )
        mine[:, pl.ds(y * deep, deep)] = scaled_stack[:, pl.ds(outer[nx - 1, y] * deep, deep)]
    for x in range(nx):
        own = halo.rows(1, False, nx * count + x, 1)
        face = jnp.where(odd[0] == 0, row(coeff, 1, x, ny - 1), own)
        put(
            pair_stack, ny + x, face * far_y[pl.ds(x * count, count), :],
            pair_rows(face * far_y[pl.ds(nx * count + x, 1), :]),
        )

    def side(y):
        for x in range(nx):
            mine[:, pl.ds((ny + x) * deep, deep)] = scaled_stack[:, pl.ds(outer[x, y] * deep, deep)]

    @pl.when(odd[0] == 0)
    def _():
        side(ny - 1)

    @pl.when(odd[0] == 1)
    def _():
        side(0)

    pairs, pairs_rhs = fold(by_rows(mine[...], pair_stack[...]), count, OF_SCALED, OF_PAIR)
    total[...] = part[...]
    total[:, pl.ds(2 * count, count)] += pairs
    total[:, pl.ds(3 * count + 2, 1)] += pairs_rhs


def shared_sums(part, scaled_stack, coeff, ya, yb, far_x, far_y):
    nx, ny, deep = coeff.shape[1:]
    wide = pltpu.VMEM((scaled_stack.shape[0], (nx + ny) * deep), BF16)
    return call(
        shared_kernel, shape(*part.shape), [VM] * 7, [wide, wide], limit=12
    )(part, scaled_stack, coeff, ya, yb, far_x, far_y)


def inverse_two(a, b, c, d):
    scale = 1.0 / (a * d - b * c)
    return d * scale, -b * scale, -c * scale, a * scale


def apply_two(matrix, first, second):
    a, b, c, d = matrix
    return a * first + b * second, c * first + d * second


def output_rows(first, second, width):
    at = lax.broadcasted_iota(jnp.int32, (EXTRA, width), 0)
    both = jnp.where(at % 2 == 0, first, second)
    high = both.astype(BF16).astype(F32)
    return jnp.where(at < 2, high, jnp.where(at < 4, both - high, 0.0))


def finish_kernel(total, inside_basis, outside_basis, inside_scaled, outside_scaled, guess, stepped):
    count = total.shape[0] - 8
    nx, ny, deep = guess.shape
    sums = total[pl.ds(0, count), :]
    level = lax.broadcasted_iota(jnp.int32, (count, 1), 0)
    lane = lax.broadcasted_iota(jnp.int32, sums.shape, 1)
    own = jnp.where(lane == level, sums, 0.0)
    of_row = lax.rsqrt(jnp.sum(own, axis=1, keepdims=True))
    of_lane = lax.rsqrt(jnp.sum(own, axis=0, keepdims=True))
    work = sums * of_row * jnp.where(lane[:1] < count, of_lane, 1.0)
    for k in range(0, count, 4):
        columns = [jnp.broadcast_to(work[:, k + b : k + b + 1], work.shape) for b in range(4)]
        rows = [work[k + a : k + a + 1, :] for a in range(4)]
        pivot = [[column[k + a : k + a + 1, :] for column in columns] for a in range(4)]
        top = inverse_two(pivot[0][0], pivot[0][1], pivot[1][0], pivot[1][1])
        line_0, line_1 = apply_two(top, rows[0], rows[1])
        across = [apply_two(top, pivot[0][b], pivot[1][b]) for b in (2, 3)]
        low = [rows[a] - pivot[a][0] * line_0 - pivot[a][1] * line_1 for a in (2, 3)]
        rest = [
            [pivot[a][b] - pivot[a][0] * across[b - 2][0] - pivot[a][1] * across[b - 2][1] for b in (2, 3)]
            for a in (2, 3)
        ]
        line_2, line_3 = apply_two(inverse_two(*rest[0], *rest[1]), *low)
        line_0 = line_0 - across[0][0] * line_2 - across[1][0] * line_3
        line_1 = line_1 - across[0][1] * line_2 - across[1][1] * line_3
        lines = (line_0, line_1, line_2, line_3)
        for a in range(4):
            work = work - columns[a] * lines[a]
        for a in range(4):
            work = jnp.where(level == k + a, lines[a], work)
    at = 3 * count
    work = work * of_row
    turned = work.T
    weights = work[:, at : at + 1]
    weights_row = turned[at : at + 1, :]
    shift_row = turned[at + 1 : at + 2, :] - jnp.sum(weights * turned[count : 2 * count, :], axis=0, keepdims=True)
    sums_row = sums.T
    rhs_row = sums_row[at + 1 : at + 2, :]
    both = jnp.sum(weights * sums, axis=0, keepdims=True)
    correction = rhs_row - both[:, count : 2 * count]
    along = jnp.sum(weights_row * (rhs_row + correction), axis=1, keepdims=True)
    tail = total[pl.ds(count, 1), :]
    size = tail[:, at + 1 : at + 2] - along
    crossing = jnp.sum(
        weights_row * (both[:, 2 * count : at] - sums_row[at + 2 : at + 3, :] - tail[:, 2 * count : at]),
        axis=1, keepdims=True,
    ) + tail[:, at + 2 : at + 3]
    lost = jnp.sum(correction * shift_row, axis=1, keepdims=True)
    step = size / (size - 2.0 * crossing - lost)
    of_basis = output_rows(weights_row, weights_row - step * shift_row, count)
    of_scaled = output_rows(jnp.zeros_like(weights_row), -step * weights_row, count)
    place = lax.broadcasted_iota(jnp.int32, (1, EXTRA), 1)
    of_rhs = jnp.where((place == OF_SCALED) | (place == OF_SCALED + 1), step, 0.0)
    of_rhs = output_rows(jnp.zeros_like(of_rhs), of_rhs, EXTRA)
    of_basis = jnp.concatenate([of_basis, of_basis], axis=1).astype(BF16)
    of_scaled = jnp.concatenate([of_scaled, of_scaled, of_rhs], axis=1).astype(BF16)
    groups = [(False, x, range(ny)) for x in (0, nx - 1)]
    for x in range(1, nx - 1):
        groups += [(True, x, range(1, ny - 1)), (False, x, (0, ny - 1))]
    starts = {True: 0, False: 0}
    order = sorted(groups, key=lambda group: not group[0])
    for within, x, places in order:
        lanes = pl.ds(starts[within] * deep, len(places) * deep)
        starts[within] += len(places)
        basis, scaled = (inside_basis, inside_scaled) if within else (outside_basis, outside_scaled)
        result = jnp.dot(of_basis, basis[:, lanes], preferred_element_type=F32)
        result += jnp.dot(of_scaled, scaled[:, lanes], preferred_element_type=F32)
        result = result[0:2] + result[2:4]
        for at, y in enumerate(places):
            guess[x, pl.ds(y, 1), :] = result[0:1, at * deep : (at + 1) * deep]
            stepped[x, pl.ds(y, 1), :] = result[1:2, at * deep : (at + 1) * deep]


def finish(total, stacks, block):
    return call(finish_kernel, (shape(*block),) * 2, [VM] * 5, limit=24)(total, *stacks)


def steps(basis, rhs, extra_diag, coeff):
    first_x, second_x, first_y, second_y, cols = faces(basis, coeff)
    first_x = swap(first_x, "gx", 0)
    second_x = swap(second_x, "gx", 1)
    first_y = swap(first_y, "gy", 0)
    second_y = swap(second_y, "gy", 1)
    results = inside(cols, coeff, rhs, extra_diag)
    inner, inside_basis, outside_basis, inside_scaled, scaled, diag, gram, square = results
    halo = (first_x, second_x, first_y, second_y)
    face_x, face_y = border(cols, inner, coeff, diag, rhs, halo)
    wide, deep = lax.axis_size("gx"), lax.axis_size("gy")
    route = []
    for i in range(wide):
        step = 1 if i % 2 else -1
        route += [(i * deep + j, i * deep + j + step) for j in range(deep) if 0 <= j + step < deep]
    far_y = lax.ppermute(face_y, ("gx", "gy"), route)
    far_x = send(face_x, "gx", -1)
    part, outside_scaled = local_sums(
        cols, inner, outside_basis, inside_scaled, scaled, gram, square, coeff, diag, rhs, halo
    )
    part = shared_sums(part, outside_scaled, coeff, first_y, second_y, far_x, far_y)
    total = sum_all(part)
    stacks = (inside_basis, outside_basis, inside_scaled, outside_scaled)
    return finish(total, stacks, rhs.shape)


def solution(mesh):
    placed = (
        P(None, "gx", "gy", None),
        P("gx", "gy", None),
        P("gx", "gy", None),
        P(None, "gx", "gy", None),
    )
    return jax.shard_map(
        steps,
        mesh=mesh,
        in_specs=placed,
        out_specs=(P("gx", "gy", None), P("gx", "gy", None)),
        check_vma=False,
    )
```

```python
import functools
import jax
import jax.numpy as jnp
from jax import lax
from jax.experimental import pallas as pl
from jax.experimental.pallas import tpu as pltpu
from jax.sharding import PartitionSpec as P

F32 = jnp.float32
BF16 = jnp.bfloat16
EXTRA = 16
LANES = 128
VM = pl.BlockSpec(memory_space=pltpu.VMEM)
RAW = pl.BlockSpec(memory_space=pl.ANY)


def shape(*dims, dtype=F32):
    return jax.ShapeDtypeStruct(dims, dtype)


def call(body, outs, ins, scratch=(), limit=24, work=0, moved=0):
    return pl.pallas_call(
        body,
        out_shape=outs,
        in_specs=ins,
        out_specs=jax.tree.map(lambda _: VM, outs),
        scratch_shapes=list(scratch),
        compiler_params=pltpu.CompilerParams(vmem_limit_bytes=limit << 20),
        cost_estimate=pl.CostEstimate(flops=work, bytes_accessed=moved, transcendentals=0),
    )


def sum_stages():
    wide, deep = lax.axis_size("gx"), lax.axis_size("gy")
    along_x = [(1 << k, 0) for k in range(wide.bit_length() - 1)]
    along_y = [(0, 1 << k) for k in range(deep.bit_length() - 1)]
    first = along_x[-2:-1] + along_y[:1]
    rest = along_y[:0:-1] + along_x[:-2] + along_x[-1:]
    groups = [first, rest[: len(rest) % 2]]
    groups += [rest[at : at + 2] for at in range(len(rest) % 2, len(rest), 2)]
    stages = []
    for group in groups:
        stage = list(group)
        if len(group) == 2:
            (a, b), (c, d) = group
            stage.append((a ^ c, b ^ d))
        stages.append(stage)
    return [stage for stage in stages if stage]


def sum_all(part):
    wide, deep = lax.axis_size("gx"), lax.axis_size("gy")
    if wide & (wide - 1) or deep & (deep - 1):
        return lax.psum(part, ("gx", "gy"))
    devices = [(i, j) for i in range(wide) for j in range(deep)]
    for stage in sum_stages():
        others = [
            lax.ppermute(
                part,
                ("gx", "gy"),
                [(i * deep + j, (i ^ a) * deep + (j ^ b)) for i, j in devices],
            )
            for a, b in stage
        ]
        for other in others:
            part = part + other
    return part


def send(block, axis, step):
    size = lax.axis_size(axis)
    return lax.ppermute(block, axis, [(i, i + step) for i in range(size) if 0 <= i + step < size])


def swap(block, axis, start):
    size = lax.axis_size(axis)
    pairs = [(i, i + 1) for i in range(start, size - 1, 2)]
    return lax.ppermute(block, axis, pairs + [(j, i) for i, j in pairs])


def halves(value):
    high = value.astype(BF16)
    return high, (value - high.astype(F32)).astype(BF16)


def put(stack, at, value, extra=None):
    count, deep = value.shape
    lanes = pl.ds(at * deep if isinstance(at, int) else pl.multiple_of(at * deep, deep), deep)
    high, low = halves(value)
    stack[pl.ds(0, count), lanes] = high
    stack[pl.ds(count, count), lanes] = low
    if extra is not None:
        stack[pl.ds(2 * count, EXTRA), lanes] = extra


def by_rows(left, right):
    return lax.dot_general(left, right, (((1,), (1,)), ((), ())), preferred_element_type=F32)


OF_RHS, OF_SCALED, OF_PAIR = 0, 2, 4


def fold(full, count, left, right):
    rows = full[:count] + full[count : 2 * count]
    if left is not None:
        at = 2 * count + left
        last = full[at : at + 1] + full[at + 1 : at + 2]
        rows = jnp.concatenate([rows, jnp.broadcast_to(last, (8, full.shape[1]))], axis=0)
    at = 2 * count + right
    return rows[:, :count] + rows[:, count : 2 * count], rows[:, at : at + 1] + rows[:, at + 1 : at + 2]


def parity():
    return lax.axis_index("gx") % 2, lax.axis_index("gy") % 2


def faces_kernel(basis, coeff, first_x, second_x, first_y, second_y, cols, slabs, sems):
    count, nx, ny, _ = basis.shape
    odd = parity()
    copies = [pltpu.make_async_copy(basis.at[:, x], slabs.at[x], sems.at[x]) for x in range(nx)]
    ends = []
    for target in (first_x, second_x):
        ends.append((coeff.at[0, nx - 1], target.at[pl.ds(ny * count, ny)]))
    for target in (first_y, second_y):
        ends.append((coeff.at[1, :, ny - 1, :], target.at[pl.ds(nx * count, nx)]))
    ends = [pltpu.make_async_copy(a, b, sems.at[nx + k]) for k, (a, b) in enumerate(ends)]
    for copy in copies + ends:
        copy.start()
    for x in range(nx):
        copies[x].wait()
        slab = jnp.swapaxes(slabs[x], 0, 1)
        cols[x] = slab
        rows = pl.ds(x * count, count)
        first_y[rows, :] = jnp.where(odd[1] == 0, slab[ny - 1], slab[0])
        second_y[rows, :] = jnp.where(odd[1] == 0, slab[0], slab[ny - 1])
    for y in range(ny):
        rows = pl.ds(y * count, count)
        first_x[rows, :] = jnp.where(odd[0] == 0, cols[nx - 1, y], cols[0, y])
        second_x[rows, :] = jnp.where(odd[0] == 0, cols[0, y], cols[nx - 1, y])
    for copy in ends:
        copy.wait()


def faces(basis, coeff):
    count, nx, ny, deep = basis.shape
    of_x, of_y = shape(ny * count + ny, deep), shape(nx * count + nx, deep)
    outs = (of_x, of_x, of_y, of_y, shape(nx, ny, count, deep))
    slabs = pltpu.VMEM((nx, count, ny, deep), F32)
    sems = pltpu.SemaphoreType.DMA((nx + 4,))
    return call(faces_kernel, outs, [RAW, RAW], [slabs, sems], limit=50)(basis, coeff)


def row(ref, *at):
    return ref[at[:-1] + (pl.ds(at[-1], 1), slice(None))]


def near_z(field, upper, lower):
    deep = field.shape[1]
    above, below = pltpu.roll(field, deep - 1, 1), pltpu.roll(field, 1, 1)
    return upper * above + lower * below


def outer_columns(nx, ny):
    ends = [(x, y) for x in range(1, nx - 1) for y in (0, ny - 1)]
    return [(x, y) for x in (0, nx - 1) for y in range(ny)] + ends


def end_rows(fields):
    parts = []
    for full in fields:
        high = full.astype(BF16).astype(F32)
        parts += [high, full - high]
    parts += [jnp.zeros_like(parts[0])] * (8 - len(parts))
    return jnp.swapaxes(jnp.stack(parts), 0, 1)


def end_block(rows):
    blank = jnp.zeros((EXTRA - rows.shape[0], rows.shape[1]), F32)
    return jnp.concatenate([rows, blank], axis=0).astype(BF16)


def inner_kernel(
    cols, coeff, rhs, extra_raw,
    inner, inside_basis, outside_basis, inside_scaled, scaled, diag, gram, square,
    upper, lower, ahead, behind, extra, ends, inside_value, sem,
):
    nx, ny, _, deep = cols.shape
    extra_copy = pltpu.make_async_copy(extra_raw, extra, sem)
    extra_copy.start()
    level = lax.broadcasted_iota(jnp.int32, (ny, deep), 0)
    lane = lax.broadcasted_iota(jnp.int32, (ny, deep), 1)
    extra_copy.wait()
    for x in range(nx):
        cx, cy, cz = coeff[0, x], coeff[1, x], coeff[2, x]
        upper[x] = jnp.where(lane == deep - 1, 0.0, cz)
        under = jnp.where(lane == 0, 0.0, pltpu.roll(cz, 1, 1))
        lower[x] = under
        before = coeff[0, x - 1] if x else jnp.zeros_like(cx)
        behind[x] = before
        ahead[x] = cx if x + 1 < nx else jnp.zeros_like(cx)
        total = extra[x] + cx + cy + cz + under + before
        diag[x] = total + jnp.where(level == 0, 0.0, pltpu.roll(cy, 1, 0))

    def slab(x, carry):
        after, before = jnp.minimum(x + 1, nx - 1), jnp.maximum(x - 1, 0)
        for y in range(ny):
            here = cols[x, y]
            sums = near_z(here, row(upper, x, y), row(lower, x, y))
            sums += row(ahead, x, y) * cols[after, y]
            sums += row(behind, x, y) * cols[before, y]
            if y + 1 < ny:
                sums += row(coeff, 1, x, y) * cols[x, y + 1]
            if y:
                sums += row(coeff, 1, x, y - 1) * cols[x, y - 1]
            inner[x, y] = row(diag, x, y) * here - sums
        return carry

    def middle(x, carry):
        scale = 1.0 / diag[x]
        ends[...] = end_rows((rhs[x], scale * rhs[x]))
        behind[x] = scale
        for y in range(1, ny - 1):
            at = (x - 1) * (ny - 2) + y - 1
            block = end_block(ends[y])
            value = inner[x, y]
            result = value * row(behind, x, y)
            scaled[x, y] = result
            put(inside_basis, at, cols[x, y])
            put(inside_value, at, value, block)
            put(inside_scaled, at, result, block)
        return carry

    lax.fori_loop(0, nx, slab, 0)
    lax.fori_loop(1, nx - 1, middle, 0)
    for at, (x, y) in enumerate(outer_columns(nx, ny)):
        put(outside_basis, at, cols[x, y])
    gram[...] = by_rows(inside_basis[...], inside_value[...])
    square[...] = by_rows(inside_value[...], inside_scaled[...])


def inside(cols, coeff, rhs, extra):
    nx, ny, count, deep = cols.shape
    cells = nx * ny * deep
    tall = 2 * count + EXTRA
    outer = len(outer_columns(nx, ny)) * deep
    full = shape(nx, ny, count, deep)
    outs = (
        full,
        shape(2 * count, cells - outer, dtype=BF16),
        shape(2 * count, outer, dtype=BF16),
        shape(tall, cells - outer, dtype=BF16),
        full,
        shape(nx, ny, deep),
        shape(2 * count, tall),
        shape(tall, tall),
    )
    small = pltpu.VMEM((nx, ny, deep), F32)
    scratch = [small] * 5 + [
        pltpu.VMEM((ny, 8, deep), F32),
        pltpu.VMEM((tall, cells - outer), BF16),
        pltpu.SemaphoreType.DMA,
    ]
    return call(
        inner_kernel, outs, [VM, VM, VM, RAW], scratch, work=60 * count * cells, moved=24 * count * cells
    )(cols, coeff, rhs, extra)


class Halo:
    def __init__(self, odd, refs):
        self.odd = odd
        self.refs = refs

    def rows(self, axis, upper, start, size):
        first, second = self.refs[2 * axis : 2 * axis + 2]
        here = pl.ds(start, size)
        return jnp.where(self.odd[axis] == (0 if upper else 1), first[here, :], second[here, :])


def inverse_diagonal(diag, halo, count, x):
    nx, ny, deep = diag.shape
    level = lax.broadcasted_iota(jnp.int32, (ny, deep), 0)
    total = diag[x] + jnp.where(level == 0, halo.rows(1, False, nx * count + x, 1), 0.0)
    if x == 0:
        total += halo.rows(0, False, ny * count, ny)
    return 1.0 / total


def full_value(cols, inner, coeff, halo, x, y):
    nx, ny, count, _ = cols.shape
    value = inner[x, y]
    if x == 0:
        value += halo.rows(0, False, ny * count + y, 1) * (cols[x, y] - halo.rows(0, False, y * count, count))
    if x == nx - 1:
        value -= row(coeff, 0, x, y) * halo.rows(0, True, y * count, count)
    if y == 0:
        value += halo.rows(1, False, nx * count + x, 1) * (cols[x, y] - halo.rows(1, False, x * count, count))
    if y == ny - 1:
        value -= row(coeff, 1, x, y) * halo.rows(1, True, x * count, count)
    return value


def border_kernel(cols, inner, coeff, diag, rhs, xa, xb, ya, yb, face_x, face_y, scale):
    nx, ny, count, _ = cols.shape
    odd = parity()
    halo = Halo(odd, (xa, xb, ya, yb))
    for x in range(nx):
        scale[x] = inverse_diagonal(diag, halo, count, x)
    value = functools.partial(full_value, cols, inner, coeff, halo)
    for y in range(ny):
        face_x[pl.ds(y * count, count), :] = value(0, y) * row(scale, 0, y)
    face_x[pl.ds(ny * count, ny), :] = scale[0] * rhs[0]

    def side(y):
        for x in range(nx):
            face_y[pl.ds(x * count, count), :] = value(x, y) * row(scale, x, y)
            face_y[pl.ds(nx * count + x, 1), :] = row(scale, x, y) * row(rhs, x, y)

    @pl.when(odd[0] == 0)
    def _():
        side(0)

    @pl.when(odd[0] == 1)
    def _():
        side(ny - 1)


def border(cols, inner, coeff, diag, rhs, halo):
    nx, ny, count, deep = cols.shape
    outs = (shape(ny * count + ny, deep), shape(nx * count + nx, deep))
    return call(
        border_kernel, outs, [VM] * 9, [pltpu.VMEM((nx, ny, deep), F32)], limit=10
    )(cols, inner, coeff, diag, rhs, *halo)


def local_kernel(
    cols, inner, outside_basis, inside_scaled, scaled, gram_in, square_in, coeff, diag, rhs, xa, xb, ya, yb,
    part, outside_scaled, outside_value, inside_pair, outside_pair, border, scale, upper, scaled_rhs, ends,
):
    nx, ny, count, deep = cols.shape
    odd = parity()
    halo = Halo(odd, (xa, xb, ya, yb))
    lane = lax.broadcasted_iota(jnp.int32, (ny, deep), 1)
    level = lax.broadcasted_iota(jnp.int32, (ny, deep), 0)
    for x in range(nx):
        inverse = inverse_diagonal(diag, halo, count, x)
        scale[x] = inverse
        scaled_rhs[x] = inverse * rhs[x]
        upper[x] = jnp.where(lane == deep - 1, 0.0, coeff[2, x])
    for x in range(nx):
        field = scaled_rhs[x]
        pair = upper[x] * pltpu.roll(field, deep - 1, 1)
        pair += jnp.where(level == ny - 1, 0.0, coeff[1, x] * pltpu.roll(field, ny - 1, 0))
        if x + 1 < nx:
            pair += coeff[0, x] * scaled_rhs[x + 1]
        ends[x] = end_rows((rhs[x], field, pair))
    outer = {place: at for at, place in enumerate(outer_columns(nx, ny))}
    for (x, y), at in outer.items():
        block = end_block(ends[x, y])
        value = full_value(cols, inner, coeff, halo, x, y)
        result = value * row(scale, x, y)
        border[at] = result
        put(outside_value, at, value, block)
        put(outside_scaled, at, result, block)

    def field_at(x, y):
        return border[outer[x, y]] if (x, y) in outer else scaled[x, y]

    for x in range(nx):
        for y in range(ny):
            pair = row(upper, x, y) * pltpu.roll(field_at(x, y), deep - 1, 1)
            if x + 1 < nx:
                pair += row(coeff, 0, x, y) * field_at(x + 1, y)
            if y + 1 < ny:
                pair += row(coeff, 1, x, y) * field_at(x, y + 1)
            block = end_block(ends[x, y])
            if (x, y) in outer:
                put(outside_pair, outer[x, y], pair, block)
            else:
                put(inside_pair, (x - 1) * (ny - 2) + y - 1, pair, block)
    gram = gram_in[...] + by_rows(outside_basis[...], outside_value[...])
    gram, projected = fold(gram, count, None, OF_RHS)
    square = square_in[...] + by_rows(outside_value[...], outside_scaled[...])
    square, square_rhs = fold(square, count, OF_RHS, OF_SCALED)
    pairs = by_rows(inside_scaled[...], inside_pair[...]) + by_rows(outside_scaled[...], outside_pair[...])
    pairs, pairs_rhs = fold(pairs, count, OF_SCALED, OF_PAIR)
    part[...] = jnp.zeros_like(part)
    part[pl.ds(0, count), pl.ds(0, count)] = gram
    part[:, pl.ds(count, count)] = square
    part[:, pl.ds(2 * count, count)] = pairs
    part[pl.ds(0, count), pl.ds(3 * count, 1)] = projected
    part[:, pl.ds(3 * count + 1, 1)] = square_rhs
    part[:, pl.ds(3 * count + 2, 1)] = pairs_rhs


def local_sums(cols, inner, outside_basis, inside_scaled, scaled, gram, square, coeff, diag, rhs, halo):
    nx, ny, count, deep = cols.shape
    cells = nx * ny * deep
    tall = 2 * count + EXTRA
    columns = len(outer_columns(nx, ny))
    outer = columns * deep
    small = pltpu.VMEM((nx, ny, deep), F32)
    width = -(-(3 * count + 3) // LANES) * LANES
    return call(
        local_kernel,
        (shape(count + 8, width), shape(tall, outer, dtype=BF16)),
        [VM] * 14,
        [
            pltpu.VMEM((tall, outer), BF16),
            pltpu.VMEM((tall, cells - outer), BF16),
            pltpu.VMEM((tall, outer), BF16),
            pltpu.VMEM((columns, count, deep), F32),
            small, small, small,
            pltpu.VMEM((nx, ny, 8, deep), F32),
        ],
        limit=28,
        work=60 * count * cells,
        moved=24 * count * cells,
    )(cols, inner, outside_basis, inside_scaled, scaled, gram, square, coeff, diag, rhs, *halo)


def pair_rows(field):
    high = field.astype(BF16).astype(F32)
    at = lax.broadcasted_iota(jnp.int32, (EXTRA, field.shape[1]), 0)
    both = jnp.where(at == OF_PAIR, high, jnp.where(at == OF_PAIR + 1, field - high, 0.0))
    return both.astype(BF16)


def shared_kernel(part, scaled_stack, coeff, ya, yb, far_x, far_y, total, mine, pair_stack):
    odd = parity()
    halo = Halo(odd, (None, None, ya, yb))
    count = part.shape[0] - 8
    nx, ny, deep = coeff.shape[1:]
    outer = {place: at for at, place in enumerate(outer_columns(nx, ny))}
    for y in range(ny):
        face = row(coeff, 0, nx - 1, y)
        put(
            pair_stack, y, face * far_x[pl.ds(y * count, count), :],
            pair_rows(face * far_x[pl.ds(ny * count + y, 1), :]),
        )
        mine[:, pl.ds(y * deep, deep)] = scaled_stack[:, pl.ds(outer[nx - 1, y] * deep, deep)]
    for x in range(nx):
        own = halo.rows(1, False, nx * count + x, 1)
        face = jnp.where(odd[0] == 0, row(coeff, 1, x, ny - 1), own)
        put(
            pair_stack, ny + x, face * far_y[pl.ds(x * count, count), :],
            pair_rows(face * far_y[pl.ds(nx * count + x, 1), :]),
        )

    def side(y):
        for x in range(nx):
            mine[:, pl.ds((ny + x) * deep, deep)] = scaled_stack[:, pl.ds(outer[x, y] * deep, deep)]

    @pl.when(odd[0] == 0)
    def _():
        side(ny - 1)

    @pl.when(odd[0] == 1)
    def _():
        side(0)

    pairs, pairs_rhs = fold(by_rows(mine[...], pair_stack[...]), count, OF_SCALED, OF_PAIR)
    total[...] = part[...]
    total[:, pl.ds(2 * count, count)] += pairs
    total[:, pl.ds(3 * count + 2, 1)] += pairs_rhs


def shared_sums(part, scaled_stack, coeff, ya, yb, far_x, far_y):
    nx, ny, deep = coeff.shape[1:]
    wide = pltpu.VMEM((scaled_stack.shape[0], (nx + ny) * deep), BF16)
    return call(
        shared_kernel, shape(*part.shape), [VM] * 7, [wide, wide], limit=12
    )(part, scaled_stack, coeff, ya, yb, far_x, far_y)


def inverse_two(a, b, c, d):
    scale = 1.0 / (a * d - b * c)
    return d * scale, -b * scale, -c * scale, a * scale


def apply_two(matrix, first, second):
    a, b, c, d = matrix
    return a * first + b * second, c * first + d * second


def output_rows(first, second, width):
    at = lax.broadcasted_iota(jnp.int32, (EXTRA, width), 0)
    both = jnp.where(at % 2 == 0, first, second)
    high = both.astype(BF16).astype(F32)
    return jnp.where(at < 2, high, jnp.where(at < 4, both - high, 0.0))


def finish_kernel(total, inside_basis, outside_basis, inside_scaled, outside_scaled, guess, stepped):
    count = total.shape[0] - 8
    nx, ny, deep = guess.shape
    sums = total[pl.ds(0, count), :]
    level = lax.broadcasted_iota(jnp.int32, (count, 1), 0)
    lane = lax.broadcasted_iota(jnp.int32, sums.shape, 1)
    own = jnp.where(lane == level, sums, 0.0)
    of_row = lax.rsqrt(jnp.sum(own, axis=1, keepdims=True))
    of_lane = lax.rsqrt(jnp.sum(own, axis=0, keepdims=True))
    work = sums * of_row * jnp.where(lane[:1] < count, of_lane, 1.0)
    for k in range(0, count, 4):
        columns = [jnp.broadcast_to(work[:, k + b : k + b + 1], work.shape) for b in range(4)]
        rows = [work[k + a : k + a + 1, :] for a in range(4)]
        pivot = [[column[k + a : k + a + 1, :] for column in columns] for a in range(4)]
        top = inverse_two(pivot[0][0], pivot[0][1], pivot[1][0], pivot[1][1])
        line_0, line_1 = apply_two(top, rows[0], rows[1])
        across = [apply_two(top, pivot[0][b], pivot[1][b]) for b in (2, 3)]
        low = [rows[a] - pivot[a][0] * line_0 - pivot[a][1] * line_1 for a in (2, 3)]
        rest = [
            [pivot[a][b] - pivot[a][0] * across[b - 2][0] - pivot[a][1] * across[b - 2][1] for b in (2, 3)]
            for a in (2, 3)
        ]
        line_2, line_3 = apply_two(inverse_two(*rest[0], *rest[1]), *low)
        line_0 = line_0 - across[0][0] * line_2 - across[1][0] * line_3
        line_1 = line_1 - across[0][1] * line_2 - across[1][1] * line_3
        lines = (line_0, line_1, line_2, line_3)
        terms = [columns[a] * lines[a] for a in range(4)]
        work = work - ((terms[0] + terms[1]) + (terms[2] + terms[3]))
        for a in range(4):
            work = jnp.where(level == k + a, lines[a], work)
    at = 3 * count
    work = work * of_row
    turned = work.T
    weights = work[:, at : at + 1]
    weights_row = turned[at : at + 1, :]
    shift_row = turned[at + 1 : at + 2, :] - jnp.sum(weights * turned[count : 2 * count, :], axis=0, keepdims=True)
    sums_row = sums.T
    rhs_row = sums_row[at + 1 : at + 2, :]
    both = jnp.sum(weights * sums, axis=0, keepdims=True)
    correction = rhs_row - both[:, count : 2 * count]
    along = jnp.sum(weights_row * (rhs_row + correction), axis=1, keepdims=True)
    tail = total[pl.ds(count, 1), :]
    size = tail[:, at + 1 : at + 2] - along
    crossing = jnp.sum(
        weights_row * (both[:, 2 * count : at] - sums_row[at + 2 : at + 3, :] - tail[:, 2 * count : at]),
        axis=1, keepdims=True,
    ) + tail[:, at + 2 : at + 3]
    lost = jnp.sum(correction * shift_row, axis=1, keepdims=True)
    step = size / (size - 2.0 * crossing - lost)
    of_basis = output_rows(weights_row, weights_row - step * shift_row, count)
    of_scaled = output_rows(jnp.zeros_like(weights_row), -step * weights_row, count)
    place = lax.broadcasted_iota(jnp.int32, (1, EXTRA), 1)
    of_rhs = jnp.where((place == OF_SCALED) | (place == OF_SCALED + 1), step, 0.0)
    of_rhs = output_rows(jnp.zeros_like(of_rhs), of_rhs, EXTRA)
    of_basis = jnp.concatenate([of_basis, of_basis], axis=1).astype(BF16)
    of_scaled = jnp.concatenate([of_scaled, of_scaled, of_rhs], axis=1).astype(BF16)
    groups = [(False, x, range(ny)) for x in (0, nx - 1)]
    for x in range(1, nx - 1):
        groups += [(True, x, range(1, ny - 1)), (False, x, (0, ny - 1))]
    starts = {True: 0, False: 0}
    order = sorted(groups, key=lambda group: not group[0])
    for within, x, places in order:
        lanes = pl.ds(starts[within] * deep, len(places) * deep)
        starts[within] += len(places)
        basis, scaled = (inside_basis, inside_scaled) if within else (outside_basis, outside_scaled)
        result = jnp.dot(of_basis, basis[:, lanes], preferred_element_type=F32)
        result += jnp.dot(of_scaled, scaled[:, lanes], preferred_element_type=F32)
        result = result[0:2] + result[2:4]
        for at, y in enumerate(places):
            guess[x, pl.ds(y, 1), :] = result[0:1, at * deep : (at + 1) * deep]
            stepped[x, pl.ds(y, 1), :] = result[1:2, at * deep : (at + 1) * deep]


def finish(total, stacks, block):
    return call(finish_kernel, (shape(*block),) * 2, [VM] * 5, limit=24)(total, *stacks)


def steps(basis, rhs, extra_diag, coeff):
    first_x, second_x, first_y, second_y, cols = faces(basis, coeff)
    first_x = swap(first_x, "gx", 0)
    second_x = swap(second_x, "gx", 1)
    first_y = swap(first_y, "gy", 0)
    second_y = swap(second_y, "gy", 1)
    results = inside(cols, coeff, rhs, extra_diag)
    inner, inside_basis, outside_basis, inside_scaled, scaled, diag, gram, square = results
    halo = (first_x, second_x, first_y, second_y)
    face_x, face_y = border(cols, inner, coeff, diag, rhs, halo)
    wide, deep = lax.axis_size("gx"), lax.axis_size("gy")
    route = []
    for i in range(wide):
        step = 1 if i % 2 else -1
        route += [(i * deep + j, i * deep + j + step) for j in range(deep) if 0 <= j + step < deep]
    far_y = lax.ppermute(face_y, ("gx", "gy"), route)
    far_x = send(face_x, "gx", -1)
    part, outside_scaled = local_sums(
        cols, inner, outside_basis, inside_scaled, scaled, gram, square, coeff, diag, rhs, halo
    )
    part = shared_sums(part, outside_scaled, coeff, first_y, second_y, far_x, far_y)
    total = sum_all(part)
    stacks = (inside_basis, outside_basis, inside_scaled, outside_scaled)
    return finish(total, stacks, rhs.shape)


def solution(mesh):
    placed = (
        P(None, "gx", "gy", None),
        P("gx", "gy", None),
        P("gx", "gy", None),
        P(None, "gx", "gy", None),
    )
    return jax.shard_map(
        steps,
        mesh=mesh,
        in_specs=placed,
        out_specs=(P("gx", "gy", None), P("gx", "gy", None)),
        check_vma=False,
    )
```
